32 devices in a mesh: dp: 8 (over z, core), ctx: 4 (over y, x).
Axes of the slice: x: 2, y: 2, z: 4, core: 2. Of those that a mesh axis runs over, the one named last changes fastest.
Arguments:
- block_input: float32 [8, 512, 1088], P('dp', 'ctx'), may hold values from -6 to 6
- block_pairs: int32 [4], replicated, may hold values from 0 to 3, each once
- attend_gain: bfloat16 [1088], P('dp'), may hold values from 0.5 to 1.5
- attend_shift: bfloat16 [1088], P('dp'), may hold values from -3 to 3
- input_weight: bfloat16 [1088, 3264], P('dp', 'ctx'), may hold values from -1 to 1
- query_bias: bfloat16 [1088], P('dp'), may hold values from -3 to 3
- value_bias: bfloat16 [1088], P('dp'), may hold values from -3 to 3
- output_weight: bfloat16 [1088, 1088], P('dp', 'ctx'), may hold values from -1.5 to 1.5
- output_bias: bfloat16 [1088], P('dp'), may hold values from -3 to 3
- feed_gain: bfloat16 [1088], P('dp'), may hold values from 0.5 to 1.5
- feed_shift: bfloat16 [1088], P('dp'), may hold values from -3 to 3
- expand_weight: bfloat16 [1088, 4352], P('dp', 'ctx'), may hold values from -0.1875 to 0.1875
- expand_bias: bfloat16 [4352], P('dp'), may hold values from -3 to 3
- reduce_weight: bfloat16 [4352, 1088], P('dp', 'ctx'), may hold values from -0.09375 to 0.09375
- reduce_bias: bfloat16 [1088], P('dp'), may hold values from -3 to 3
- output_cotangent: float32 [8, 512, 1088], P('dp', 'ctx'), may hold values from -6 to 6
Outputs:
- block_output: float32 [8, 512, 1088], P('dp', 'ctx')
- input_grad: float32 [8, 512, 1088], P('dp', 'ctx')
- grad_attend_gain: float32 [1088], P('dp')
- grad_attend_shift: float32 [1088], P('dp')
- grad_input_weight: float32 [1088, 3264], P('dp', 'ctx')
- grad_query_bias: float32 [1088], P('dp')
- grad_value_bias: float32 [1088], P('dp')
- grad_output_weight: float32 [1088, 1088], P('dp', 'ctx')
- grad_output_bias: float32 [1088], P('dp')
- grad_feed_gain: float32 [1088], P('dp')
- grad_feed_shift: float32 [1088], P('dp')
- grad_expand_weight: float32 [1088, 4352], P('dp', 'ctx')
- grad_expand_bias: float32 [4352], P('dp')
- grad_reduce_weight: float32 [4352, 1088], P('dp', 'ctx')
- grad_reduce_bias: float32 [1088], P('dp')
The draws below stay inside these ranges and needn't reach their ends.
Inputs may be any that keep to these rules, and one draw needn't show every extreme that they name: `block_pairs`: each number from 0 to 3 appears once.
All inputs are finite; a program needn't handle non-finite values.
Results may differ from the reference program's by a relative error of at most 0.012.
The reference program's roundings to bfloat16 on the way count: a program that leaves them out, or rounds other values in their place, can miss the bound.
Values may be sent and summed in bfloat16 or wider, within the bound.
No kernel may reach another device: no remote copies, remote signals or barrier semaphores. Data moves between devices by JAX's collectives and lax.ppermute only.
A program may use at most 256 MiB of HBM per device.

```python
import jax
import jax.numpy as jnp
from jax import lax

D = 1088
HEADS = 17
HEAD_DIM = 64
FF = 4352
BLK = 64
PAIRS = 4
LENGTH = 512
SEQS = 8


def draw_input_weight(key, part):
    matrix = jax.random.normal(key, (D, 3 * D), jnp.float32) * D ** (-0.5)
    return jnp.clip(matrix, -1.0, 1.0).astype(jnp.bfloat16)


def level_of(own_key, shape, shards, smallest, top_value):
    level, own = 1.0, jax.random.fold_in(own_key, 6)
    for axis_at, blocks in shards:
        heights = jnp.exp(jax.random.uniform(jax.random.fold_in(own, axis_at), (blocks,), jnp.float32, smallest / len(shards), top_value / len(shards)))
        level = level * jnp.repeat(heights, shape[axis_at] // blocks).reshape([-1 if axis == axis_at else 1 for axis in range(len(shape))])
    return level


def noise(own_key, shape, deviation, reach, shards=(), kind=jnp.bfloat16):
    values = deviation * jax.random.normal(own_key, shape, jnp.float32)
    if shards:
        values = values * level_of(own_key, shape, shards, -0.22, 0.18)
    return jnp.clip(values, -reach, reach).astype(kind)


def setup_inputs(seed: int = 0) -> dict:
    splits = jax.random.split(jax.random.key(seed), 17)
    block_input = noise(splits[0], (SEQS, LENGTH, D), 1.0, 6.0, ((0, 8), (1, 4)), jnp.float32)
    block_pairs = jax.random.permutation(splits[1], PAIRS).astype(jnp.int32)
    attend_gain = jnp.clip(1.0 + 0.1 * jax.random.normal(splits[2], (D,), jnp.float32), 0.5, 1.5).astype(jnp.bfloat16)
    attend_shift = noise(splits[3], (D,), 0.5, 3.0, ((0, 8),))
    input_weight = draw_input_weight(jax.random.fold_in(splits[16], 71), 0)
    query_bias = noise(splits[5], (D,), 0.5, 3.0, ((0, 8),))
    value_bias = noise(splits[6], (D,), 0.5, 3.0, ((0, 8),))
    output_weight = noise(splits[7], (D, D), (D // 64) ** -0.5, 1.5, ((0, 8), (1, 4)))
    output_bias = noise(splits[8], (D,), 0.5, 3.0, ((0, 8),))
    feed_gain = jnp.clip(1.0 + 0.1 * jax.random.normal(splits[9], (D,), jnp.float32), 0.5, 1.5).astype(jnp.bfloat16)
    feed_shift = noise(splits[10], (D,), 0.5, 3.0, ((0, 8),))
    expand_weight = noise(splits[11], (D, FF), D ** -0.5, 0.1875, ((0, 8), (1, 4)))
    expand_bias = noise(splits[12], (FF,), 0.5, 3.0, ((0, 8),))
    reduce_weight = noise(splits[13], (FF, D), FF ** -0.5, 0.09375, ((0, 8), (1, 4)))
    reduce_bias = noise(splits[14], (D,), 0.5, 3.0, ((0, 8),))
    output_cotangent = noise(splits[15], (SEQS, LENGTH, D), 1.0, 6.0, ((0, 8), (1, 4)), jnp.float32)
    return {"block_input": block_input, "block_pairs": block_pairs, "attend_gain": attend_gain, "attend_shift": attend_shift, "input_weight": input_weight, "query_bias": query_bias, "value_bias": value_bias, "output_weight": output_weight, "output_bias": output_bias, "feed_gain": feed_gain, "feed_shift": feed_shift, "expand_weight": expand_weight, "expand_bias": expand_bias, "reduce_weight": reduce_weight, "reduce_bias": reduce_bias, "output_cotangent": output_cotangent}


EPSILON = 1e-05
GELU_ROOT = 0.7978845608028654
GELU_CUBIC = 0.044715
MASKED = -1e+30

def layer_norm(matrix, norm_gain, norm_shift):
    average = lax.optimization_barrier(jnp.mean(matrix, axis=-1, keepdims=True))
    centered = matrix - average
    variance = lax.optimization_barrier(jnp.mean(centered * centered, axis=-1, keepdims=True))
    inverse = lax.rsqrt(variance + EPSILON)
    normed = centered * inverse
    return (normed * norm_gain.astype(jnp.float32) + norm_shift.astype(jnp.float32), normed, inverse)

def norm_backward(upstream, normed, inverse, norm_gain):
    grad_gain = lax.optimization_barrier(jnp.sum(upstream * normed, axis=0))
    grad_shift = lax.optimization_barrier(jnp.sum(upstream, axis=0))
    scaled = upstream * norm_gain.astype(jnp.float32)
    centred_grad = scaled - lax.optimization_barrier(jnp.mean(scaled, axis=-1, keepdims=True)) - normed * lax.optimization_barrier(jnp.mean(scaled * normed, axis=-1, keepdims=True))
    return (inverse * centred_grad, grad_gain, grad_shift)

def gelu_pair(before):
    cubic = GELU_ROOT * (before + GELU_CUBIC * before * before * before)
    tangent = jnp.tanh(cubic)
    result = 0.5 * before * (1.0 + tangent)
    derivative = 0.5 * (1.0 + tangent) + 0.5 * before * (1.0 - tangent * tangent) * GELU_ROOT * (1.0 + 3.0 * GELU_CUBIC * before * before)
    return (result, derivative)

def token_positions(block_pairs):
    stored = jnp.arange(LENGTH, dtype=jnp.int32)
    slot_index = stored // (2 * BLK)
    within = stored % (2 * BLK)
    owner_pair = block_pairs[slot_index].astype(jnp.int32)
    first_half = owner_pair * BLK + within
    second_half = (2 * PAIRS - 1 - owner_pair) * BLK + within - BLK
    return jnp.where(within < BLK, first_half, second_half).astype(jnp.int32)

def masked_scores(queries, keys, query_pos, key_pos):
    count = queries.shape[0]
    query_heads = queries.reshape(count, HEADS, HEAD_DIM).astype(jnp.float32)
    key_heads = keys.reshape(keys.shape[0], HEADS, HEAD_DIM).astype(jnp.float32)
    scores = jnp.einsum('rhe,lhe->hrl', query_heads, key_heads) * HEAD_DIM ** (-0.5)
    allowed = key_pos[None, None, :] <= query_pos[None, :, None]
    return jnp.where(allowed, scores, MASKED)

def attention_forward(queries, keys, values, query_pos, key_pos):
    count = queries.shape[0]
    scores = masked_scores(queries, keys, query_pos, key_pos)
    highest = lax.optimization_barrier(jnp.max(scores, axis=-1, keepdims=True))
    log_total = highest + jnp.log(lax.optimization_barrier(jnp.sum(jnp.exp(scores - highest), axis=-1, keepdims=True)))
    probs = jnp.exp(scores - log_total).astype(jnp.bfloat16)
    value_heads = values.reshape(values.shape[0], HEADS, HEAD_DIM).astype(jnp.float32)
    mixed = jnp.einsum('hrl,lhe->rhe', probs.astype(jnp.float32), value_heads)
    return (mixed.reshape(count, D).astype(jnp.bfloat16), log_total)

def attention_backward(queries, keys, values, query_pos, key_pos, log_total, mixed, grad_mixed):
    count = queries.shape[0]
    scores = masked_scores(queries, keys, query_pos, key_pos)
    exact = jnp.exp(scores - log_total)
    probs = exact.astype(jnp.bfloat16).astype(jnp.float32)
    query_heads = queries.reshape(count, HEADS, HEAD_DIM).astype(jnp.float32)
    key_heads = keys.reshape(keys.shape[0], HEADS, HEAD_DIM).astype(jnp.float32)
    value_heads = values.reshape(values.shape[0], HEADS, HEAD_DIM).astype(jnp.float32)
    grad_heads = grad_mixed.reshape(count, HEADS, HEAD_DIM).astype(jnp.float32)
    mixed_heads = mixed.reshape(count, HEADS, HEAD_DIM).astype(jnp.float32)
    grad_values = jnp.einsum('hrl,rhe->lhe', probs, grad_heads)
    grad_probs = jnp.einsum('rhe,lhe->hrl', grad_heads, value_heads)
    delta = lax.optimization_barrier(jnp.sum(grad_heads * mixed_heads, axis=-1)).T
    grad_scores = (exact * (grad_probs - delta[:, :, None]) * HEAD_DIM ** (-0.5)).astype(jnp.bfloat16).astype(jnp.float32)
    grad_queries = jnp.einsum('hrl,lhe->rhe', grad_scores, key_heads)
    grad_keys = jnp.einsum('hrl,rhe->lhe', grad_scores, query_heads)
    total = keys.shape[0]
    return (grad_queries.reshape(count, D), grad_keys.reshape(total, D), grad_values.reshape(total, D))

def sequence_pass(inputs, cotangent, weights, positions, query_block, block_count):
    attend_gain, attend_shift, input_weight, query_bias, value_bias, output_weight, output_bias, feed_gain, feed_shift, expand_weight, expand_bias, reduce_weight, reduce_bias = weights
    normed_in, first_normed, first_inverse = layer_norm(inputs, attend_gain, attend_shift)
    attend_in = normed_in.astype(jnp.bfloat16)
    projected = jnp.dot(attend_in, input_weight, preferred_element_type=jnp.float32)
    queries = (projected[:, :D] + query_bias.astype(jnp.float32)).astype(jnp.bfloat16)
    keys = projected[:, D:2 * D].astype(jnp.bfloat16)
    values = (projected[:, 2 * D:] + value_bias.astype(jnp.float32)).astype(jnp.bfloat16)
    query_blocks = queries.reshape(block_count, query_block, D)
    position_blocks = positions.reshape(block_count, query_block)

    def forward_block(pieces):
        return attention_forward(pieces[0], keys, values, pieces[1], positions)
    mixed_blocks, log_blocks = lax.map(forward_block, (query_blocks, position_blocks))
    mixed = mixed_blocks.reshape(LENGTH, D)
    resid = inputs + jnp.dot(mixed, output_weight, preferred_element_type=jnp.float32) + output_bias.astype(jnp.float32)
    normed_mid, second_normed, second_inverse = layer_norm(resid, feed_gain, feed_shift)
    feed_in = normed_mid.astype(jnp.bfloat16)
    before = jnp.dot(feed_in, expand_weight, preferred_element_type=jnp.float32) + expand_bias.astype(jnp.float32)
    activated, slope = gelu_pair(before)
    activ_low = activated.astype(jnp.bfloat16)
    output = resid + jnp.dot(activ_low, reduce_weight, preferred_element_type=jnp.float32) + reduce_bias.astype(jnp.float32)
    cot_low = cotangent.astype(jnp.bfloat16)
    grad_reduce_weight = jnp.dot(activ_low.T, cot_low, preferred_element_type=jnp.float32)
    grad_reduce_bias = lax.optimization_barrier(jnp.sum(cotangent, axis=0))
    grad_before = jnp.dot(cot_low, reduce_weight.T, preferred_element_type=jnp.float32) * slope
    before_low = grad_before.astype(jnp.bfloat16)
    grad_expand_weight = jnp.dot(feed_in.T, before_low, preferred_element_type=jnp.float32)
    grad_expand_bias = lax.optimization_barrier(jnp.sum(grad_before, axis=0))
    grad_feed_in = jnp.dot(before_low, expand_weight.T, preferred_element_type=jnp.float32)
    grad_mid, grad_feed_gain, grad_feed_shift = norm_backward(grad_feed_in, second_normed, second_inverse, feed_gain)
    grad_resid = cotangent + grad_mid
    resid_low = grad_resid.astype(jnp.bfloat16)
    grad_output_weight = jnp.dot(mixed.T, resid_low, preferred_element_type=jnp.float32)
    grad_output_bias = lax.optimization_barrier(jnp.sum(grad_resid, axis=0))
    grad_mixed = jnp.dot(resid_low, output_weight.T, preferred_element_type=jnp.float32).astype(jnp.bfloat16)
    grad_blocks = grad_mixed.reshape(block_count, query_block, D)

    def backward_block(carry, pieces):
        block_query, block_pos, block_log, block_mixed, block_grad = pieces
        grad_query, grad_key, grad_value = attention_backward(block_query, keys, values, block_pos, positions, block_log, block_mixed, block_grad)
        return ((carry[0] + grad_key, carry[1] + grad_value), grad_query)
    start_sums = (jnp.zeros((LENGTH, D), jnp.float32), jnp.zeros((LENGTH, D), jnp.float32))
    (grad_keys, grad_values), grad_query_blocks = lax.scan(backward_block, start_sums, (query_blocks, position_blocks, log_blocks, mixed_blocks, grad_blocks))
    grad_queries = grad_query_blocks.reshape(LENGTH, D)
    grad_query_bias = lax.optimization_barrier(jnp.sum(grad_queries, axis=0))
    grad_value_bias = lax.optimization_barrier(jnp.sum(grad_values, axis=0))
    grad_proj = jnp.concatenate([grad_queries, grad_keys, grad_values], axis=1).astype(jnp.bfloat16)
    grad_input_weight = jnp.dot(attend_in.T, grad_proj, preferred_element_type=jnp.float32)
    grad_attend_in = jnp.dot(grad_proj, input_weight.T, preferred_element_type=jnp.float32)
    grad_first, grad_attend_gain, grad_attend_shift = norm_backward(grad_attend_in, first_normed, first_inverse, attend_gain)
    input_grad = grad_resid + grad_first
    grads = (grad_attend_gain, grad_attend_shift, grad_input_weight, grad_query_bias, grad_value_bias, grad_output_weight, grad_output_bias, grad_feed_gain, grad_feed_shift, grad_expand_weight, grad_expand_bias, grad_reduce_weight, grad_reduce_bias)
    return (output, input_grad, grads)

def reference(block_input, block_pairs, attend_gain, attend_shift, input_weight, query_bias, value_bias, output_weight, output_bias, feed_gain, feed_shift, expand_weight, expand_bias, reduce_weight, reduce_bias, output_cotangent):
    positions = token_positions(block_pairs)
    query_block = min(512, LENGTH)
    block_count = LENGTH // query_block
    weights = (attend_gain, attend_shift, input_weight, query_bias, value_bias, output_weight, output_bias, feed_gain, feed_shift, expand_weight, expand_bias, reduce_weight, reduce_bias)
    zero_sums = tuple((jnp.zeros(weight_piece.shape, jnp.float32) for weight_piece in weights))

    def one_sequence(totals, pieces):
        output, input_grad, grads = sequence_pass(pieces[0], pieces[1], weights, positions, query_block, block_count)
        return (tuple((total_term + new_term for total_term, new_term in zip(totals, grads))), (output, input_grad))
    totals, (outputs, input_grads) = lax.scan(one_sequence, zero_sums, (block_input, output_cotangent))
    grad_attend_gain, grad_attend_shift, grad_input_weight, grad_query_bias, grad_value_bias, grad_output_weight, grad_output_bias, grad_feed_gain, grad_feed_shift, grad_expand_weight, grad_expand_bias, grad_reduce_weight, grad_reduce_bias = totals
    return (outputs, input_grads, grad_attend_gain, grad_attend_shift, grad_input_weight, grad_query_bias, grad_value_bias, grad_output_weight, grad_output_bias, grad_feed_gain, grad_feed_shift, grad_expand_weight, grad_expand_bias, grad_reduce_weight, grad_reduce_bias)
```

```python
import numpy as np

import jax
import jax.numpy as jnp
from jax import lax
from jax.experimental import pallas as pl
from jax.experimental.pallas import tpu as pltpu
from jax.sharding import PartitionSpec as P

HEADS = 17
HEAD_DIM = 64

EPSILON = 1e-05
GELU_ROOT = 0.7978845608028654
GELU_CUBIC = 0.044715
MASKED = -1e30

BF = jnp.bfloat16
F32 = jnp.float32


def layer_norm(matrix, norm_gain, norm_shift):
    average = jnp.mean(matrix, axis=-1, keepdims=True)
    centered = matrix - average
    variance = jnp.mean(centered * centered, axis=-1, keepdims=True)
    inverse = lax.rsqrt(variance + EPSILON)
    normed = centered * inverse
    return (normed * norm_gain + norm_shift, normed, inverse)


def norm_backward(upstream, normed, inverse, norm_gain):
    grad_gain = jnp.sum(upstream * normed, axis=0)
    grad_shift = jnp.sum(upstream, axis=0)
    scaled = upstream * norm_gain
    centred_grad = (
        scaled
        - jnp.mean(scaled, axis=-1, keepdims=True)
        - normed * jnp.mean(scaled * normed, axis=-1, keepdims=True)
    )
    return (inverse * centred_grad, grad_gain, grad_shift)


def gelu_pair(before):
    cubic = GELU_ROOT * (before + GELU_CUBIC * before * before * before)
    tangent = jnp.tanh(cubic)
    result = 0.5 * before * (1.0 + tangent)
    derivative = 0.5 * (1.0 + tangent) + 0.5 * before * (1.0 - tangent * tangent) * GELU_ROOT * (
        1.0 + 3.0 * GELU_CUBIC * before * before
    )
    return (result, derivative)


def mm(left, right):
    return jnp.dot(left, right, preferred_element_type=F32)


def mm_nt(left, right):
    return lax.dot_general(left, right, (((1,), (1,)), ((), ())), preferred_element_type=F32)


def mm_tn(left, right):
    return lax.dot_general(left, right, (((0,), (0,)), ((), ())), preferred_element_type=F32)


def shuffle(blocks, me):
    blocks = list(blocks)
    step = 1
    while step < len(blocks):
        odd = (me // step) % 2 == 1
        blocks = [
            jnp.where(odd, blocks[at ^ step], blocks[at]) for at in range(len(blocks))
        ]
        step *= 2
    return blocks


def swap_with(value, axis, step):
    count = lax.axis_size(axis)
    return lax.ppermute(value, axis, [(at, at ^ step) for at in range(count)])


def exchange(blocks, axis):
    return [blocks[0]] + [
        swap_with(blocks[step], axis, step) for step in range(1, len(blocks))
    ]


def gather_rel(value, axis):
    return exchange([value] * lax.axis_size(axis), axis)


def reduce_rows(partial, axis):
    count = lax.axis_size(axis)
    rows = partial.shape[0] // count
    total = partial[:rows]
    for step in range(1, count):
        piece = partial[step * rows : (step + 1) * rows].astype(BF)
        total = total + swap_with(piece, axis, step).astype(F32)
    return total


def dp_reduce(grad, cores=2):
    count = lax.axis_size("dp")
    levels = count // cores
    index = lax.axis_index("dp")
    rows = grad.shape[0] // count
    width = grad.shape[1]
    view = grad.reshape(levels, cores, rows, width)
    core = index % cores
    keep = jnp.where(core == 0, view[:, 0], view[:, 1])
    away = jnp.where(core == 0, view[:, 1], view[:, 0]).astype(BF)
    keep = keep + swap_with(away, "dp", 1).astype(F32)
    blocks = shuffle([keep[at] for at in range(levels)], index // cores)
    total = blocks[0]
    for step in range(1, levels):
        total = total + swap_with(blocks[step].astype(BF), "dp", step * cores).astype(F32)
    return total


def head_tables(count, width, own_heads):
    share = own_heads * HEAD_DIM
    columns = 3 * width // count
    lists = {}
    most = 1
    for target in range(count):
        for place in range(3 * share):
            part, inner = divmod(place, share)
            column = target * share + inner
            if column < width:
                source, local = divmod(part * width + column, columns)
                lists.setdefault((source, target), []).append((local, place))
    most = max(len(entries) for entries in lists.values())
    send = np.full((count, count, most), -1, np.int32)
    put = np.full((count, count, most), -1, np.int32)
    for (source, target), entries in lists.items():
        for at, (local, place) in enumerate(entries):
            send[source, source ^ target, at] = local
            put[target, source ^ target, at] = place
    return send.reshape(count, -1), put.reshape(count, -1), most


def scores_of(query, key, row_pos, col_pos):
    score = mm_nt(query, key) * (HEAD_DIM ** (-0.5))
    return jnp.where(col_pos <= row_pos, score, MASKED)


def attend_kernel(own_heads, chunk, qkv_ref, row_ref, col_ref, mixed_ref, log_ref):
    rows = qkv_ref.shape[0]
    share = own_heads * HEAD_DIM
    col_pos = col_ref[...]
    for head in range(own_heads):
        span = slice(head * HEAD_DIM, (head + 1) * HEAD_DIM)
        key = qkv_ref[:, share + head * HEAD_DIM : share + (head + 1) * HEAD_DIM]
        value = qkv_ref[:, 2 * share + head * HEAD_DIM : 2 * share + (head + 1) * HEAD_DIM]
        for first in range(0, rows, chunk):
            part = slice(first, first + chunk)
            score = scores_of(qkv_ref[part, span], key, row_ref[part, :], col_pos)
            top = jnp.max(score, axis=-1, keepdims=True)
            log = top + jnp.log(jnp.sum(jnp.exp(score - top), axis=-1, keepdims=True))
            probs = jnp.exp(score - log).astype(BF)
            mixed_ref[part, span] = mm(probs, value).astype(BF)
            log_ref[part, head : head + 1] = log


def attend_back_kernel(
    own_heads, chunk, qkv_ref, row_ref, col_ref, log_ref, mixed_ref, grad_ref, out_ref, bias_ref
):
    rows = qkv_ref.shape[0]
    share = own_heads * HEAD_DIM
    scale = HEAD_DIM ** (-0.5)
    col_pos = col_ref[...]
    for head in range(own_heads):
        span = slice(head * HEAD_DIM, (head + 1) * HEAD_DIM)
        key_span = slice(share + head * HEAD_DIM, share + (head + 1) * HEAD_DIM)
        value_span = slice(2 * share + head * HEAD_DIM, 2 * share + (head + 1) * HEAD_DIM)
        key = qkv_ref[:, key_span]
        value = qkv_ref[:, value_span]
        grad_key = grad_value = grad_query_sum = None
        for first in range(0, rows, chunk):
            part = slice(first, first + chunk)
            query = qkv_ref[part, span]
            score = scores_of(query, key, row_ref[part, :], col_pos)
            exact = jnp.exp(score - log_ref[part, head : head + 1])
            grad = grad_ref[part, span]
            delta = jnp.sum(
                grad.astype(F32) * mixed_ref[part, span].astype(F32), axis=-1, keepdims=True
            )
            new_value = mm_tn(exact.astype(BF), grad)
            grad_score = (exact * (mm_nt(grad, value) - delta) * scale).astype(BF)
            grad_query = mm(grad_score, key)
            new_key = mm_tn(grad_score, query)
            new_sum = jnp.sum(grad_query, axis=0, keepdims=True)
            out_ref[part, span] = grad_query.astype(BF)
            if first == 0:
                grad_key, grad_value, grad_query_sum = new_key, new_value, new_sum
            else:
                grad_key = grad_key + new_key
                grad_value = grad_value + new_value
                grad_query_sum = grad_query_sum + new_sum
        out_ref[:, key_span] = grad_key.astype(BF)
        out_ref[:, value_span] = grad_value.astype(BF)
        bias_ref[0:1, span] = grad_query_sum
        bias_ref[1:2, span] = jnp.sum(grad_value, axis=0, keepdims=True)


def attend_forward(qkv, row_pos, col_pos, own_heads, chunk):
    rows = qkv.shape[0]
    return pl.pallas_call(
        lambda *refs: attend_kernel(own_heads, chunk, *refs),
        out_shape=(
            jax.ShapeDtypeStruct((rows, own_heads * HEAD_DIM), BF),
            jax.ShapeDtypeStruct((rows, own_heads), F32),
        ),
        name="attend",
    )(qkv, row_pos, col_pos)


def attend_backward(qkv, row_pos, col_pos, log, mixed, grad, own_heads, chunk):
    rows = qkv.shape[0]
    return pl.pallas_call(
        lambda *refs: attend_back_kernel(own_heads, chunk, *refs),
        out_shape=(
            jax.ShapeDtypeStruct((rows, 3 * own_heads * HEAD_DIM), BF),
            jax.ShapeDtypeStruct((2, own_heads * HEAD_DIM), F32),
        ),
        name="attend_back",
    )(qkv, row_pos, col_pos, log, mixed, grad)


def body(
    block_input,
    block_pairs,
    attend_gain,
    attend_shift,
    input_weight,
    query_bias,
    value_bias,
    output_weight,
    output_bias,
    feed_gain,
    feed_shift,
    expand_weight,
    expand_bias,
    reduce_weight,
    reduce_bias,
    output_cotangent,
):
    inputs = block_input[0]
    cotangent = output_cotangent[0]
    rows, width = inputs.shape
    count = lax.axis_size("ctx")
    groups = lax.axis_size("dp")
    me = lax.axis_index("ctx")
    half = rows // 2
    own_heads = -(-HEADS // count)
    share = own_heads * HEAD_DIM
    padded = share * count
    shard_rows = input_weight.shape[0]
    shard_columns = output_weight.shape[1]
    hidden = reduce_weight.shape[0] * groups
    unit = hidden // (groups * count)
    hidden_share = hidden // count
    spans = groups // count
    chunk = min(rows * count, (1 << 18) // (rows * count))

    own_expand_bias = lax.dynamic_slice_in_dim(expand_bias, me * unit, unit)
    small = jnp.stack(
        [
            attend_gain,
            attend_shift,
            query_bias,
            value_bias,
            output_bias,
            feed_gain,
            feed_shift,
            reduce_bias,
        ]
    )
    both = jnp.concatenate([small.reshape(-1), own_expand_bias])
    gathered = shuffle(gather_rel(both, "dp"), lax.axis_index("dp"))
    cut = 8 * shard_rows
    vectors = jnp.stack([piece[:cut].reshape(8, shard_rows) for piece in gathered], axis=1)
    vectors = vectors.reshape(8, width).astype(F32)
    own_expand = jnp.concatenate([piece[cut:] for piece in gathered]).astype(F32)
    pad = padded - width
    own_query_bias = lax.dynamic_slice_in_dim(jnp.pad(vectors[2], (0, pad)), me * share, share)
    own_value_bias = lax.dynamic_slice_in_dim(jnp.pad(vectors[3], (0, pad)), me * share, share)
    proj_bias = jnp.concatenate([own_query_bias, jnp.zeros((share,), F32), own_value_bias])

    send_table, put_table, most = head_tables(count, width, own_heads)
    send_at = lax.dynamic_index_in_dim(jnp.asarray(send_table), me, keepdims=False)
    put_at = lax.dynamic_index_in_dim(jnp.asarray(put_table), me, keepdims=False)
    pick = (lax.broadcasted_iota(jnp.int32, (input_weight.shape[1], count * most), 0)
            == send_at[None, :]).astype(BF)
    place = (lax.broadcasted_iota(jnp.int32, (count * most, 3 * share), 1)
             == put_at[:, None]).astype(BF)
    picked = mm(input_weight, pick).astype(BF)
    arrived = exchange(
        [picked[:, step * most : (step + 1) * most] for step in range(count)], "ctx"
    )
    own_input = mm(jnp.concatenate(arrived, axis=1), place).astype(BF)
    full_input = lax.all_gather(own_input, "dp", axis=0, tiled=True)

    output_parts = shuffle(gather_rel(output_weight, "ctx"), me)
    full_output = lax.all_gather(
        jnp.concatenate(output_parts, axis=1), "dp", axis=0, tiled=True
    )
    expand_view = expand_weight.reshape(shard_rows, spans, count, unit)
    expand_parts = shuffle(
        exchange(
            shuffle(
                [
                    expand_view[:, :, at].reshape(shard_rows, spans * unit)
                    for at in range(count)
                ],
                me,
            ),
            "ctx",
        ),
        me,
    )
    full_expand = lax.all_gather(
        jnp.concatenate(expand_parts, axis=1), "dp", axis=0, tiled=True
    )
    reduce_view = reduce_weight.reshape(count, unit, shard_columns)
    reduce_parts = shuffle(
        exchange(shuffle([reduce_view[at] for at in range(count)], me), "ctx"), me
    )
    full_reduce = lax.all_gather(
        jnp.concatenate(reduce_parts, axis=1), "dp", axis=0, tiled=True
    )

    pair_list = shuffle([block_pairs[at] for at in range(count)], me)
    inner = jnp.arange(half, dtype=jnp.int32)
    positions = jnp.concatenate(
        [
            piece
            for pair in pair_list
            for piece in (pair * half + inner, (2 * count - 1 - pair) * half + inner)
        ]
    )
    row_pos = positions[:, None]
    col_pos = positions[None, :]

    normed_in, first_normed, first_inverse = layer_norm(inputs, vectors[0], vectors[1])
    attend_in = normed_in.astype(BF)
    attend_all = jnp.concatenate(gather_rel(attend_in, "ctx"))
    cot_low = cotangent.astype(BF)
    cot_all = jnp.concatenate(gather_rel(cot_low, "ctx"))
    qkv = (mm(attend_all, full_input) + proj_bias).astype(BF)
    own_mixed, log = attend_forward(qkv, row_pos, col_pos, own_heads, chunk)
    mixed_parts = shuffle(
        exchange([own_mixed[at * rows : (at + 1) * rows] for at in range(count)], "ctx"), me
    )
    mixed = jnp.concatenate(mixed_parts, axis=1)[:, :width]
    resid = inputs + mm(mixed, full_output) + vectors[4]
    normed_mid, second_normed, second_inverse = layer_norm(resid, vectors[5], vectors[6])
    feed_in = normed_mid.astype(BF)
    feed_all = jnp.concatenate(gather_rel(feed_in, "ctx"))
    before = mm(feed_all, full_expand) + own_expand
    activated, slope = gelu_pair(before)
    activ_low = activated.astype(BF)

    grad_before = mm_nt(cot_all, full_reduce) * slope
    before_low = grad_before.astype(BF)
    grad_expand_bias = jnp.sum(grad_before, axis=0)
    grad_feed_in = reduce_rows(mm_nt(before_low, full_expand), "ctx")
    output = resid + reduce_rows(mm(activ_low, full_reduce), "ctx") + vectors[7]
    grad_mid, grad_feed_gain, grad_feed_shift = norm_backward(
        grad_feed_in, second_normed, second_inverse, vectors[5]
    )
    grad_resid = cotangent + grad_mid
    resid_low = grad_resid.astype(BF)
    grad_mixed = jnp.pad(mm_nt(resid_low, full_output).astype(BF), ((0, 0), (0, pad)))
    own_grad_mixed = jnp.concatenate(
        exchange(
            shuffle([grad_mixed[:, at * share : (at + 1) * share] for at in range(count)], me),
            "ctx",
        )
    )
    grad_reduce = dp_reduce(mm_tn(activ_low, cot_all))
    grad_expand = dp_reduce(mm_tn(feed_all, before_low))
    mixed_all = jnp.concatenate(gather_rel(mixed, "ctx"))
    resid_cols = jnp.concatenate(
        exchange(
            shuffle(
                [
                    resid_low[:, at * shard_columns : (at + 1) * shard_columns]
                    for at in range(count)
                ],
                me,
            ),
            "ctx",
        )
    )
    grad_output_weight = dp_reduce(mm_tn(mixed_all, resid_cols))

    grad_proj, proj_sums = attend_backward(
        qkv, row_pos, col_pos, log, own_mixed, own_grad_mixed, own_heads, chunk
    )
    grad_attend_in = reduce_rows(mm_nt(grad_proj, full_input), "ctx")
    grad_first, grad_attend_gain, grad_attend_shift = norm_backward(
        grad_attend_in, first_normed, first_inverse, vectors[0]
    )
    input_grad = grad_resid + grad_first
    grad_input = dp_reduce(mm_tn(attend_all, grad_proj)).astype(BF)

    back_input = mm_nt(grad_input, place).astype(BF)
    back_input = exchange(
        [back_input[:, step * most : (step + 1) * most] for step in range(count)], "ctx"
    )
    grad_input_weight = mm_nt(jnp.concatenate(back_input, axis=1), pick)
    back_reduce = grad_reduce.astype(BF)
    back_reduce = shuffle(
        exchange(
            shuffle(
                [
                    back_reduce[:, at * shard_columns : (at + 1) * shard_columns]
                    for at in range(count)
                ],
                me,
            ),
            "ctx",
        ),
        me,
    )
    grad_reduce_weight = jnp.concatenate(back_reduce, axis=0).astype(F32)
    back_expand = grad_expand.astype(BF)
    back_expand = shuffle(
        exchange(
            shuffle(
                [
                    back_expand[:, at * spans * unit : (at + 1) * spans * unit]
                    for at in range(count)
                ],
                me,
            ),
            "ctx",
        ),
        me,
    )
    grad_expand_weight = jnp.stack(
        [piece.reshape(shard_rows, spans, unit) for piece in back_expand], axis=2
    ).reshape(shard_rows, spans * count * unit).astype(F32)

    def widen(piece):
        whole = lax.dynamic_update_slice(jnp.zeros((padded,), F32), piece, (me * share,))
        return whole[:width]

    stacked = jnp.stack(
        [
            grad_attend_gain,
            grad_attend_shift,
            widen(proj_sums[0]),
            widen(proj_sums[1]),
            jnp.sum(grad_resid, axis=0),
            grad_feed_gain,
            grad_feed_shift,
            jnp.sum(cotangent, axis=0),
        ]
    )
    slots = (jnp.arange(count) == me).astype(F32)
    hidden_sums = grad_expand_bias.reshape(groups, 1, unit) * slots[None, :, None]
    vector_rows = stacked.reshape(8, groups, shard_rows).transpose(1, 0, 2).reshape(groups, -1)
    all_rows = jnp.concatenate([vector_rows, hidden_sums.reshape(groups, -1)], axis=1)
    dp_blocks = exchange(
        shuffle([all_rows[at] for at in range(groups)], lax.axis_index("dp")), "dp"
    )
    dp_total = sum(dp_blocks[1:], dp_blocks[0])
    ctx_blocks = gather_rel(dp_total, "ctx")
    total = sum(ctx_blocks[1:], ctx_blocks[0])
    sums = total[:cut].reshape(8, shard_rows)
    return (
        output[None],
        input_grad[None],
        sums[0],
        sums[1],
        grad_input_weight,
        sums[2],
        sums[3],
        grad_output_weight,
        sums[4],
        sums[5],
        sums[6],
        grad_expand_weight,
        total[cut:],
        grad_reduce_weight,
        sums[7],
    )


def solution(mesh):
    matrix = P("dp", "ctx")
    vector = P("dp")
    tokens = P("dp", "ctx", None)
    return jax.shard_map(
        body,
        mesh=mesh,
        in_specs=(
            tokens,
            P(),
            vector,
            vector,
            matrix,
            vector,
            vector,
            matrix,
            vector,
            vector,
            vector,
            matrix,
            vector,
            matrix,
            vector,
            tokens,
        ),
        out_specs=(
            tokens,
            tokens,
            vector,
            vector,
            matrix,
            vector,
            vector,
            matrix,
            vector,
            vector,
            vector,
            matrix,
            vector,
            matrix,
            vector,
        ),
        check_vma=False,
    )
```

```python
import numpy as np

import jax
import jax.numpy as jnp
from jax import lax
from jax.experimental import pallas as pl
from jax.experimental.pallas import tpu as pltpu
from jax.sharding import PartitionSpec as P

HEADS = 17
HEAD_DIM = 64

EPSILON = 1e-05
GELU_ROOT = 0.7978845608028654
GELU_CUBIC = 0.044715
MASKED = -1e30
CORES = 2

BF = jnp.bfloat16
F32 = jnp.float32


def layer_norm(matrix, norm_gain, norm_shift):
    average = jnp.mean(matrix, axis=-1, keepdims=True)
    centered = matrix - average
    variance = jnp.mean(centered * centered, axis=-1, keepdims=True)
    inverse = lax.rsqrt(variance + EPSILON)
    normed = centered * inverse
    return (normed * norm_gain + norm_shift, normed, inverse)


def norm_backward(upstream, normed, inverse, norm_gain):
    grad_gain = jnp.sum(upstream * normed, axis=0)
    grad_shift = jnp.sum(upstream, axis=0)
    scaled = upstream * norm_gain
    centred_grad = (
        scaled
        - jnp.mean(scaled, axis=-1, keepdims=True)
        - normed * jnp.mean(scaled * normed, axis=-1, keepdims=True)
    )
    return (inverse * centred_grad, grad_gain, grad_shift)


def gelu_pair(before):
    cubic = GELU_ROOT * (before + GELU_CUBIC * before * before * before)
    tangent = jnp.tanh(cubic)
    result = 0.5 * before * (1.0 + tangent)
    derivative = 0.5 * (1.0 + tangent) + 0.5 * before * (1.0 - tangent * tangent) * GELU_ROOT * (
        1.0 + 3.0 * GELU_CUBIC * before * before
    )
    return (result, derivative)


def mm(left, right):
    return jnp.dot(left, right, preferred_element_type=F32)


def mm_nt(left, right):
    return lax.dot_general(left, right, (((1,), (1,)), ((), ())), preferred_element_type=F32)


def mm_tn(left, right):
    return lax.dot_general(left, right, (((0,), (0,)), ((), ())), preferred_element_type=F32)


def shuffle(blocks, me):
    blocks = list(blocks)
    step = 1
    while step < len(blocks):
        odd = (me // step) % 2 == 1
        blocks = [
            jnp.where(odd, blocks[at ^ step], blocks[at]) for at in range(len(blocks))
        ]
        step *= 2
    return blocks


def swap_with(value, axis, step):
    count = lax.axis_size(axis)
    return lax.ppermute(value, axis, [(at, at ^ step) for at in range(count)])


def exchange(blocks, axis):
    return [blocks[0]] + [
        swap_with(blocks[step], axis, step) for step in range(1, len(blocks))
    ]


def gather_rel(value, axis):
    return exchange([value] * lax.axis_size(axis), axis)


def reduce_rows(partial, axis):
    count = lax.axis_size(axis)
    rows = partial.shape[0] // count
    total = partial[:rows]
    for step in range(1, count):
        piece = partial[step * rows : (step + 1) * rows].astype(BF)
        total = total + swap_with(piece, axis, step).astype(F32)
    return total


def level_pairs(pairs):
    return [(CORES * a + core, CORES * b + core) for a, b in pairs for core in range(CORES)]


def place_of_dp():
    index = lax.axis_index("dp")
    return index // CORES, index % CORES, lax.axis_size("dp") // CORES


def gather_levels(value):
    level, _, levels = place_of_dp()
    if levels == 4:
        near = swap_with(value, "dp", CORES)
        far = swap_with(value, "dp", 2 * CORES)
        middle = lax.ppermute(value, "dp", level_pairs([(1, 2), (2, 1)]))
        onward = lax.ppermute(far, "dp", level_pairs([(2, 3), (1, 0)]))
        last = jnp.where((level == 1) | (level == 2), middle, onward)
        blocks = [value, near, far, last]
    else:
        blocks = [value] + [swap_with(value, "dp", CORES * step) for step in range(1, levels)]
    return jnp.stack(shuffle(blocks, level))


def gather_dp(value):
    _, core, levels = place_of_dp()
    mine = gather_levels(value)
    other = swap_with(mine, "dp", 1)
    first = jnp.where(core == 0, mine, other)
    second = jnp.where(core == 0, other, mine)
    return jnp.stack([first, second], axis=1).reshape((CORES * levels,) + value.shape)


def reduce_cores(grads):
    level, core, levels = place_of_dp()
    keeps, aways = [], []
    for grad in grads:
        rows = grad.shape[0] // (levels * CORES)
        view = grad.reshape(levels, CORES, rows, grad.shape[1])
        keeps.append(jnp.where(core == 0, view[:, 0], view[:, 1]))
        aways.append(jnp.where(core == 0, view[:, 1], view[:, 0]).astype(BF))
    other = swap_with(jnp.concatenate(aways, axis=1), "dp", 1)
    keep = jnp.concatenate(keeps, axis=1) + other.astype(F32)
    return shuffle([keep[at] for at in range(levels)], level)


def reduce_levels(blocks):
    levels = len(blocks)
    if levels == 4:
        ahead = lax.ppermute(blocks[3].astype(BF), "dp", level_pairs([(3, 2), (0, 1)]))
        near = swap_with(blocks[1].astype(BF), "dp", CORES)
        middle = lax.ppermute(blocks[3].astype(BF), "dp", level_pairs([(1, 2), (2, 1)]))
        far = swap_with((blocks[2] + ahead.astype(F32)).astype(BF), "dp", 2 * CORES)
        return blocks[0] + near.astype(F32) + middle.astype(F32) + far.astype(F32)
    total = blocks[0]
    for step in range(1, levels):
        total = total + swap_with(blocks[step].astype(BF), "dp", step * CORES).astype(F32)
    return total


def head_tables(count, width, own_heads):
    share = own_heads * HEAD_DIM
    columns = 3 * width // count
    lists = {}
    most = 1
    for target in range(count):
        for place in range(3 * share):
            part, inner = divmod(place, share)
            column = target * share + inner
            if column < width:
                source, local = divmod(part * width + column, columns)
                lists.setdefault((source, target), []).append((local, place))
    most = max(len(entries) for entries in lists.values())
    send = np.full((count, count, most), -1, np.int32)
    put = np.full((count, count, most), -1, np.int32)
    for (source, target), entries in lists.items():
        for at, (local, place) in enumerate(entries):
            send[source, source ^ target, at] = local
            put[target, source ^ target, at] = place
    return send.reshape(count, -1), put.reshape(count, -1), most


def scores_of(query, key, row_pos, col_pos):
    score = mm_nt(query, key) * (HEAD_DIM ** (-0.5))
    return jnp.where(col_pos <= row_pos, score, MASKED)


def attend_kernel(own_heads, chunk, qkv_ref, row_ref, col_ref, mixed_ref, log_ref):
    rows = qkv_ref.shape[0]
    share = own_heads * HEAD_DIM
    col_pos = col_ref[...]
    for head in range(own_heads):
        span = slice(head * HEAD_DIM, (head + 1) * HEAD_DIM)
        key = qkv_ref[:, share + head * HEAD_DIM : share + (head + 1) * HEAD_DIM]
        value = qkv_ref[:, 2 * share + head * HEAD_DIM : 2 * share + (head + 1) * HEAD_DIM]
        for first in range(0, rows, chunk):
            part = slice(first, first + chunk)
            score = scores_of(qkv_ref[part, span], key, row_ref[part, :], col_pos)
            top = jnp.max(score, axis=-1, keepdims=True)
            log = top + jnp.log(jnp.sum(jnp.exp(score - top), axis=-1, keepdims=True))
            probs = jnp.exp(score - log).astype(BF)
            mixed_ref[part, span] = mm(probs, value).astype(BF)
            log_ref[part, head : head + 1] = log


def attend_back_kernel(
    own_heads, chunk, qkv_ref, row_ref, col_ref, log_ref, mixed_ref, grad_ref, out_ref, bias_ref
):
    rows = qkv_ref.shape[0]
    share = own_heads * HEAD_DIM
    scale = HEAD_DIM ** (-0.5)
    col_pos = col_ref[...]
    for head in range(own_heads):
        span = slice(head * HEAD_DIM, (head + 1) * HEAD_DIM)
        key_span = slice(share + head * HEAD_DIM, share + (head + 1) * HEAD_DIM)
        value_span = slice(2 * share + head * HEAD_DIM, 2 * share + (head + 1) * HEAD_DIM)
        key = qkv_ref[:, key_span]
        value = qkv_ref[:, value_span]
        grad_key = grad_value = grad_query_sum = None
        for first in range(0, rows, chunk):
            part = slice(first, first + chunk)
            query = qkv_ref[part, span]
            score = scores_of(query, key, row_ref[part, :], col_pos)
            exact = jnp.exp(score - log_ref[part, head : head + 1])
            grad = grad_ref[part, span]
            delta = jnp.sum(
                grad.astype(F32) * mixed_ref[part, span].astype(F32), axis=-1, keepdims=True
            )
            new_value = mm_tn(exact.astype(BF), grad)
            grad_score = (exact * (mm_nt(grad, value) - delta) * scale).astype(BF)
            grad_query = mm(grad_score, key)
            new_key = mm_tn(grad_score, query)
            new_sum = jnp.sum(grad_query, axis=0, keepdims=True)
            out_ref[part, span] = grad_query.astype(BF)
            if first == 0:
                grad_key, grad_value, grad_query_sum = new_key, new_value, new_sum
            else:
                grad_key = grad_key + new_key
                grad_value = grad_value + new_value
                grad_query_sum = grad_query_sum + new_sum
        out_ref[:, key_span] = grad_key.astype(BF)
        out_ref[:, value_span] = grad_value.astype(BF)
        bias_ref[0:1, span] = grad_query_sum
        bias_ref[1:2, span] = jnp.sum(grad_value, axis=0, keepdims=True)


def attend_forward(qkv, row_pos, col_pos, own_heads, chunk):
    rows = qkv.shape[0]
    return pl.pallas_call(
        lambda *refs: attend_kernel(own_heads, chunk, *refs),
        out_shape=(
            jax.ShapeDtypeStruct((rows, own_heads * HEAD_DIM), BF),
            jax.ShapeDtypeStruct((rows, own_heads), F32),
        ),
        name="attend",
    )(qkv, row_pos, col_pos)


def attend_backward(qkv, row_pos, col_pos, log, mixed, grad, own_heads, chunk):
    rows = qkv.shape[0]
    return pl.pallas_call(
        lambda *refs: attend_back_kernel(own_heads, chunk, *refs),
        out_shape=(
            jax.ShapeDtypeStruct((rows, 3 * own_heads * HEAD_DIM), BF),
            jax.ShapeDtypeStruct((2, own_heads * HEAD_DIM), F32),
        ),
        name="attend_back",
    )(qkv, row_pos, col_pos, log, mixed, grad)


def body(
    block_input,
    block_pairs,
    attend_gain,
    attend_shift,
    input_weight,
    query_bias,
    value_bias,
    output_weight,
    output_bias,
    feed_gain,
    feed_shift,
    expand_weight,
    expand_bias,
    reduce_weight,
    reduce_bias,
    output_cotangent,
):
    inputs = block_input[0]
    cotangent = output_cotangent[0]
    rows, width = inputs.shape
    count = lax.axis_size("ctx")
    groups = lax.axis_size("dp")
    me = lax.axis_index("ctx")
    half = rows // 2
    own_heads = -(-HEADS // count)
    share = own_heads * HEAD_DIM
    padded = share * count
    shard_rows = input_weight.shape[0]
    shard_columns = output_weight.shape[1]
    hidden = reduce_weight.shape[0] * groups
    unit = hidden // (groups * count)
    hidden_share = hidden // count
    spans = groups // count
    chunk = min(rows * count, (1 << 18) // (rows * count))

    own_expand_bias = lax.dynamic_slice_in_dim(expand_bias, me * unit, unit)
    small = jnp.stack(
        [
            attend_gain,
            attend_shift,
            query_bias,
            value_bias,
            output_bias,
            feed_gain,
            feed_shift,
            reduce_bias,
        ]
    )
    both = jnp.concatenate([small.reshape(-1), own_expand_bias])
    gathered = gather_dp(both)
    cut = 8 * shard_rows
    vectors = gathered[:, :cut].reshape(groups, 8, shard_rows).transpose(1, 0, 2)
    vectors = vectors.reshape(8, width).astype(F32)
    own_expand = gathered[:, cut:].reshape(hidden_share).astype(F32)
    pad = padded - width
    own_query_bias = lax.dynamic_slice_in_dim(jnp.pad(vectors[2], (0, pad)), me * share, share)
    own_value_bias = lax.dynamic_slice_in_dim(jnp.pad(vectors[3], (0, pad)), me * share, share)
    proj_bias = jnp.concatenate([own_query_bias, jnp.zeros((share,), F32), own_value_bias])

    send_table, put_table, most = head_tables(count, width, own_heads)
    send_at = lax.dynamic_index_in_dim(jnp.asarray(send_table), me, keepdims=False)
    put_at = lax.dynamic_index_in_dim(jnp.asarray(put_table), me, keepdims=False)
    pick = (lax.broadcasted_iota(jnp.int32, (input_weight.shape[1], count * most), 0)
            == send_at[None, :]).astype(BF)
    place = (lax.broadcasted_iota(jnp.int32, (count * most, 3 * share), 1)
             == put_at[:, None]).astype(BF)
    picked = mm(input_weight, pick).astype(BF)
    arrived = exchange(
        [picked[:, step * most : (step + 1) * most] for step in range(count)], "ctx"
    )
    own_input = mm(jnp.concatenate(arrived, axis=1), place).astype(BF)
    full_input = gather_dp(own_input).reshape(width, 3 * share)

    expand_view = expand_weight.reshape(shard_rows, spans, count, unit)
    expand_parts = [
        expand_view[:, :, at].reshape(shard_rows, spans * unit) for at in range(count)
    ]
    reduce_view = reduce_weight.reshape(count, unit, shard_columns)
    if unit == shard_rows and spans * unit == shard_columns:
        packs = [
            jnp.stack([output_weight, expand_part, reduce_view[at]])
            for at, expand_part in enumerate(expand_parts)
        ]
        packs = shuffle(exchange(shuffle(packs, me), "ctx"), me)
        joined = jnp.concatenate(packs, axis=2)
        own_output, own_pair = joined[0], joined[1:]
        full_output = gather_dp(own_output).reshape(width, width)
        full_pair = gather_dp(own_pair)
        full_expand = full_pair[:, 0].reshape(width, hidden_share)
        full_reduce = full_pair[:, 1].reshape(hidden_share, width)
    else:
        output_parts = shuffle(gather_rel(output_weight, "ctx"), me)
        full_output = gather_dp(jnp.concatenate(output_parts, axis=1)).reshape(width, width)
        expand_parts = shuffle(exchange(shuffle(expand_parts, me), "ctx"), me)
        full_expand = gather_dp(jnp.concatenate(expand_parts, axis=1))
        full_expand = full_expand.reshape(width, hidden_share)
        reduce_parts = shuffle([reduce_view[at] for at in range(count)], me)
        reduce_parts = shuffle(exchange(reduce_parts, "ctx"), me)
        full_reduce = gather_dp(jnp.concatenate(reduce_parts, axis=1))
        full_reduce = full_reduce.reshape(hidden_share, width)

    pair_list = shuffle([block_pairs[at] for at in range(count)], me)
    inner = jnp.arange(half, dtype=jnp.int32)
    positions = jnp.concatenate(
        [
            piece
            for pair in pair_list
            for piece in (pair * half + inner, (2 * count - 1 - pair) * half + inner)
        ]
    )
    row_pos = positions[:, None]
    col_pos = positions[None, :]

    normed_in, first_normed, first_inverse = layer_norm(inputs, vectors[0], vectors[1])
    attend_in = normed_in.astype(BF)
    attend_all = jnp.concatenate(gather_rel(attend_in, "ctx"))
    cot_low = cotangent.astype(BF)
    cot_all = jnp.concatenate(gather_rel(cot_low, "ctx"))
    qkv = (mm(attend_all, full_input) + proj_bias).astype(BF)
    own_mixed, log = attend_forward(qkv, row_pos, col_pos, own_heads, chunk)
    mixed_parts = shuffle(
        exchange([own_mixed[at * rows : (at + 1) * rows] for at in range(count)], "ctx"), me
    )
    mixed = jnp.concatenate(mixed_parts, axis=1)[:, :width]
    resid = inputs + mm(mixed, full_output) + vectors[4]
    normed_mid, second_normed, second_inverse = layer_norm(resid, vectors[5], vectors[6])
    feed_in = normed_mid.astype(BF)
    feed_all = jnp.concatenate(gather_rel(feed_in, "ctx"))
    before = mm(feed_all, full_expand) + own_expand
    activated, slope = gelu_pair(before)
    activ_low = activated.astype(BF)

    grad_before = mm_nt(cot_all, full_reduce) * slope
    before_low = grad_before.astype(BF)
    grad_expand_bias = jnp.sum(grad_before, axis=0)
    grad_feed_in = reduce_rows(mm_nt(before_low, full_expand), "ctx")
    output = resid + reduce_rows(mm(activ_low, full_reduce), "ctx") + vectors[7]
    grad_mid, grad_feed_gain, grad_feed_shift = norm_backward(
        grad_feed_in, second_normed, second_inverse, vectors[5]
    )
    grad_resid = cotangent + grad_mid
    resid_low = grad_resid.astype(BF)
    grad_mixed = jnp.pad(mm_nt(resid_low, full_output).astype(BF), ((0, 0), (0, pad)))
    own_grad_mixed = jnp.concatenate(
        exchange(
            shuffle([grad_mixed[:, at * share : (at + 1) * share] for at in range(count)], me),
            "ctx",
        )
    )
    pair_grads = (mm_tn(activ_low, cot_all), mm_tn(feed_all, before_low))
    paired = pair_grads[0].shape == pair_grads[1].shape
    if paired:
        pair_blocks = [reduce_cores(pair_grads)]
    else:
        pair_blocks = [reduce_cores(pair_grads[:1]), reduce_cores(pair_grads[1:])]
    own_grad_mixed, pair_blocks = lax.optimization_barrier((own_grad_mixed, pair_blocks))
    pair_totals = [reduce_levels(blocks) for blocks in pair_blocks]
    if paired:
        pair_totals = [pair_totals[0][:unit], pair_totals[0][unit:]]
    grad_reduce, grad_expand = pair_totals
    mixed_all = jnp.concatenate(gather_rel(mixed, "ctx"))
    resid_cols = jnp.concatenate(
        exchange(
            shuffle(
                [
                    resid_low[:, at * shard_columns : (at + 1) * shard_columns]
                    for at in range(count)
                ],
                me,
            ),
            "ctx",
        )
    )
    grad_output_weight = reduce_levels(reduce_cores([mm_tn(mixed_all, resid_cols)]))

    grad_proj, proj_sums = attend_backward(
        qkv, row_pos, col_pos, log, own_mixed, own_grad_mixed, own_heads, chunk
    )
    grad_input = reduce_levels(reduce_cores([mm_tn(attend_all, grad_proj)])).astype(BF)
    grad_attend_in = reduce_rows(mm_nt(grad_proj, full_input), "ctx")
    grad_first, grad_attend_gain, grad_attend_shift = norm_backward(
        grad_attend_in, first_normed, first_inverse, vectors[0]
    )
    input_grad = grad_resid + grad_first

    back_input = mm_nt(grad_input, place).astype(BF)
    back_input = exchange(
        [back_input[:, step * most : (step + 1) * most] for step in range(count)], "ctx"
    )
    grad_input_weight = mm_nt(jnp.concatenate(back_input, axis=1), pick)
    back_reduce = grad_reduce.astype(BF)
    back_reduce = [
        back_reduce[:, at * shard_columns : (at + 1) * shard_columns] for at in range(count)
    ]
    back_expand = grad_expand.astype(BF)
    back_expand = [
        back_expand[:, at * spans * unit : (at + 1) * spans * unit] for at in range(count)
    ]
    if paired and spans * unit == shard_columns:
        backs = [jnp.stack(pair) for pair in zip(back_reduce, back_expand)]
        backs = shuffle(exchange(shuffle(backs, me), "ctx"), me)
        back_reduce = [piece[0] for piece in backs]
        back_expand = [piece[1] for piece in backs]
    else:
        back_reduce = shuffle(exchange(shuffle(back_reduce, me), "ctx"), me)
        back_expand = shuffle(exchange(shuffle(back_expand, me), "ctx"), me)
    grad_reduce_weight = jnp.concatenate(back_reduce, axis=0).astype(F32)
    grad_expand_weight = (
        jnp.stack([piece.reshape(shard_rows, spans, unit) for piece in back_expand], axis=2)
        .reshape(shard_rows, spans * count * unit)
        .astype(F32)
    )

    def widen(piece):
        whole = lax.dynamic_update_slice(jnp.zeros((padded,), F32), piece, (me * share,))
        return whole[:width]

    stacked = jnp.stack(
        [
            grad_attend_gain,
            grad_attend_shift,
            widen(proj_sums[0]),
            widen(proj_sums[1]),
            jnp.sum(grad_resid, axis=0),
            grad_feed_gain,
            grad_feed_shift,
            jnp.sum(cotangent, axis=0),
        ]
    )
    slots = (jnp.arange(count) == me).astype(F32)
    hidden_sums = grad_expand_bias.reshape(groups, 1, unit) * slots[None, :, None]
    vector_rows = stacked.reshape(8, groups, shard_rows).transpose(1, 0, 2).reshape(groups, -1)
    all_rows = jnp.concatenate([vector_rows, hidden_sums.reshape(groups, -1)], axis=1)
    level, core, levels = place_of_dp()
    by_core = all_rows.reshape(levels, CORES, -1)
    dp_sum = jnp.where(core == 0, by_core[:, 0], by_core[:, 1]) + swap_with(
        jnp.where(core == 0, by_core[:, 1], by_core[:, 0]), "dp", 1
    )
    dp_blocks = shuffle([dp_sum[at] for at in range(levels)], level)
    dp_total = dp_blocks[0]
    for step in range(1, levels):
        dp_total = dp_total + swap_with(dp_blocks[step], "dp", step * CORES)
    ctx_blocks = gather_rel(dp_total, "ctx")
    total = sum(ctx_blocks[1:], ctx_blocks[0])
    sums = total[:cut].reshape(8, shard_rows)
    return (
        output[None],
        input_grad[None],
        sums[0],
        sums[1],
        grad_input_weight,
        sums[2],
        sums[3],
        grad_output_weight,
        sums[4],
        sums[5],
        sums[6],
        grad_expand_weight,
        total[cut:],
        grad_reduce_weight,
        sums[7],
    )


def solution(mesh):
    matrix = P("dp", "ctx")
    vector = P("dp")
    tokens = P("dp", "ctx", None)
    return jax.shard_map(
        body,
        mesh=mesh,
        in_specs=(
            tokens,
            P(),
            vector,
            vector,
            matrix,
            vector,
            vector,
            matrix,
            vector,
            vector,
            vector,
            matrix,
            vector,
            matrix,
            vector,
            tokens,
        ),
        out_specs=(
            tokens,
            tokens,
            vector,
            vector,
            matrix,
            vector,
            vector,
            matrix,
            vector,
            vector,
            vector,
            matrix,
            vector,
            matrix,
            vector,
        ),
        check_vma=False,
    )
```

```python
import numpy as np

import jax
import jax.numpy as jnp
from jax import lax
from jax.experimental import pallas as pl
from jax.experimental.pallas import tpu as pltpu
from jax.sharding import PartitionSpec as P

HEADS = 17
HEAD_DIM = 64

EPSILON = 1e-05
GELU_ROOT = 0.7978845608028654
GELU_CUBIC = 0.044715
MASKED = -1e30
CORES = 2

BF = jnp.bfloat16
F32 = jnp.float32


def layer_norm(matrix, norm_gain, norm_shift):
    average = jnp.mean(matrix, axis=-1, keepdims=True)
    centered = matrix - average
    variance = jnp.mean(centered * centered, axis=-1, keepdims=True)
    inverse = lax.rsqrt(variance + EPSILON)
    normed = centered * inverse
    return (normed * norm_gain + norm_shift, normed, inverse)


def norm_backward(upstream, normed, inverse, norm_gain):
    grad_gain = jnp.sum(upstream * normed, axis=0)
    grad_shift = jnp.sum(upstream, axis=0)
    scaled = upstream * norm_gain
    centred_grad = (
        scaled
        - jnp.mean(scaled, axis=-1, keepdims=True)
        - normed * jnp.mean(scaled * normed, axis=-1, keepdims=True)
    )
    return (inverse * centred_grad, grad_gain, grad_shift)


def gelu_pair(before):
    cubic = GELU_ROOT * (before + GELU_CUBIC * before * before * before)
    tangent = jnp.tanh(cubic)
    result = 0.5 * before * (1.0 + tangent)
    derivative = 0.5 * (1.0 + tangent) + 0.5 * before * (1.0 - tangent * tangent) * GELU_ROOT * (
        1.0 + 3.0 * GELU_CUBIC * before * before
    )
    return (result, derivative)


def mm(left, right):
    return jnp.dot(left, right, preferred_element_type=F32)


def mm_nt(left, right):
    return lax.dot_general(left, right, (((1,), (1,)), ((), ())), preferred_element_type=F32)


def mm_tn(left, right):
    return lax.dot_general(left, right, (((0,), (0,)), ((), ())), preferred_element_type=F32)


def shuffle(blocks, me):
    blocks = list(blocks)
    step = 1
    while step < len(blocks):
        odd = (me // step) % 2 == 1
        blocks = [
            jnp.where(odd, blocks[at ^ step], blocks[at]) for at in range(len(blocks))
        ]
        step *= 2
    return blocks


def swap_with(value, axis, step):
    count = lax.axis_size(axis)
    return lax.ppermute(value, axis, [(at, at ^ step) for at in range(count)])


def exchange(blocks, axis):
    return [blocks[0]] + [
        swap_with(blocks[step], axis, step) for step in range(1, len(blocks))
    ]


def gather_rel(value, axis):
    return exchange([value] * lax.axis_size(axis), axis)


def reduce_rows(partial, axis):
    count = lax.axis_size(axis)
    rows = partial.shape[0] // count
    total = partial[:rows]
    for step in range(1, count):
        piece = partial[step * rows : (step + 1) * rows].astype(BF)
        total = total + swap_with(piece, axis, step).astype(F32)
    return total


def place_of_dp():
    index = lax.axis_index("dp")
    return index // CORES, index % CORES, lax.axis_size("dp") // CORES


def gather_levels(value):
    level, _, levels = place_of_dp()
    blocks = [value] + [swap_with(value, "dp", CORES * step) for step in range(1, levels)]
    return jnp.stack(shuffle(blocks, level))


def gather_dp(value):
    _, core, levels = place_of_dp()
    mine = gather_levels(value)
    other = swap_with(mine, "dp", 1)
    first = jnp.where(core == 0, mine, other)
    second = jnp.where(core == 0, other, mine)
    return jnp.stack([first, second], axis=1).reshape((CORES * levels,) + value.shape)


def split_cores(grad):
    _, core, levels = place_of_dp()
    view = grad.reshape(levels, CORES, -1, grad.shape[1])
    keep = jnp.where(core == 0, view[:, 0], view[:, 1])
    away = jnp.where(core == 0, view[:, 1], view[:, 0]).astype(BF)
    return keep, away


def sum_cores(keep, away):
    level, _, levels = place_of_dp()
    keep = keep + swap_with(away, "dp", 1).astype(F32)
    blocks = shuffle([keep[at] for at in range(levels)], level)
    return blocks[:1] + [block.astype(BF) for block in blocks[1:]]


def sum_levels(blocks):
    total = blocks[0]
    for step in range(1, len(blocks)):
        total = total + swap_with(blocks[step], "dp", step * CORES).astype(F32)
    return total


def head_tables(count, width, own_heads):
    share = own_heads * HEAD_DIM
    columns = 3 * width // count
    lists = {}
    most = 1
    for target in range(count):
        for place in range(3 * share):
            part, inner = divmod(place, share)
            column = target * share + inner
            if column < width:
                source, local = divmod(part * width + column, columns)
                lists.setdefault((source, target), []).append((local, place))
    most = max(len(entries) for entries in lists.values())
    send = np.full((count, count, most), -1, np.int32)
    put = np.full((count, count, most), -1, np.int32)
    for (source, target), entries in lists.items():
        for at, (local, place) in enumerate(entries):
            send[source, source ^ target, at] = local
            put[target, source ^ target, at] = place
    return send.reshape(count, -1), put.reshape(count, -1), most


def scores_of(query, key, row_pos, col_pos):
    score = mm_nt(query, key) * (HEAD_DIM ** (-0.5))
    return jnp.where(col_pos <= row_pos, score, MASKED)


def attend_kernel(own_heads, chunk, qkv_ref, row_ref, col_ref, mixed_ref, log_ref):
    rows = qkv_ref.shape[0]
    share = own_heads * HEAD_DIM
    col_pos = col_ref[...]
    for head in range(own_heads):
        span = slice(head * HEAD_DIM, (head + 1) * HEAD_DIM)
        key = qkv_ref[:, share + head * HEAD_DIM : share + (head + 1) * HEAD_DIM]
        value = qkv_ref[:, 2 * share + head * HEAD_DIM : 2 * share + (head + 1) * HEAD_DIM]
        for first in range(0, rows, chunk):
            part = slice(first, first + chunk)
            score = scores_of(qkv_ref[part, span], key, row_ref[part, :], col_pos)
            top = jnp.max(score, axis=-1, keepdims=True)
            log = top + jnp.log(jnp.sum(jnp.exp(score - top), axis=-1, keepdims=True))
            probs = jnp.exp(score - log).astype(BF)
            mixed_ref[part, span] = mm(probs, value).astype(BF)
            log_ref[part, head : head + 1] = log


def attend_back_kernel(
    own_heads, chunk, qkv_ref, row_ref, col_ref, log_ref, mixed_ref, grad_ref, out_ref, bias_ref
):
    rows = qkv_ref.shape[0]
    share = own_heads * HEAD_DIM
    scale = HEAD_DIM ** (-0.5)
    col_pos = col_ref[...]
    for head in range(own_heads):
        span = slice(head * HEAD_DIM, (head + 1) * HEAD_DIM)
        key_span = slice(share + head * HEAD_DIM, share + (head + 1) * HEAD_DIM)
        value_span = slice(2 * share + head * HEAD_DIM, 2 * share + (head + 1) * HEAD_DIM)
        key = qkv_ref[:, key_span]
        value = qkv_ref[:, value_span]
        grad_key = grad_value = grad_query_sum = None
        for first in range(0, rows, chunk):
            part = slice(first, first + chunk)
            query = qkv_ref[part, span]
            score = scores_of(query, key, row_ref[part, :], col_pos)
            exact = jnp.exp(score - log_ref[part, head : head + 1])
            grad = grad_ref[part, span]
            delta = jnp.sum(
                grad.astype(F32) * mixed_ref[part, span].astype(F32), axis=-1, keepdims=True
            )
            new_value = mm_tn(exact.astype(BF), grad)
            grad_score = (exact * (mm_nt(grad, value) - delta) * scale).astype(BF)
            grad_query = mm(grad_score, key)
            new_key = mm_tn(grad_score, query)
            new_sum = jnp.sum(grad_query, axis=0, keepdims=True)
            out_ref[part, span] = grad_query.astype(BF)
            if first == 0:
                grad_key, grad_value, grad_query_sum = new_key, new_value, new_sum
            else:
                grad_key = grad_key + new_key
                grad_value = grad_value + new_value
                grad_query_sum = grad_query_sum + new_sum
        out_ref[:, key_span] = grad_key.astype(BF)
        out_ref[:, value_span] = grad_value.astype(BF)
        bias_ref[0:1, span] = grad_query_sum
        bias_ref[1:2, span] = jnp.sum(grad_value, axis=0, keepdims=True)


def attend_forward(qkv, row_pos, col_pos, own_heads, chunk):
    rows = qkv.shape[0]
    return pl.pallas_call(
        lambda *refs: attend_kernel(own_heads, chunk, *refs),
        out_shape=(
            jax.ShapeDtypeStruct((rows, own_heads * HEAD_DIM), BF),
            jax.ShapeDtypeStruct((rows, own_heads), F32),
        ),
        name="attend",
    )(qkv, row_pos, col_pos)


def attend_backward(qkv, row_pos, col_pos, log, mixed, grad, own_heads, chunk):
    rows = qkv.shape[0]
    return pl.pallas_call(
        lambda *refs: attend_back_kernel(own_heads, chunk, *refs),
        out_shape=(
            jax.ShapeDtypeStruct((rows, 3 * own_heads * HEAD_DIM), BF),
            jax.ShapeDtypeStruct((2, own_heads * HEAD_DIM), F32),
        ),
        name="attend_back",
    )(qkv, row_pos, col_pos, log, mixed, grad)


def body(
    block_input,
    block_pairs,
    attend_gain,
    attend_shift,
    input_weight,
    query_bias,
    value_bias,
    output_weight,
    output_bias,
    feed_gain,
    feed_shift,
    expand_weight,
    expand_bias,
    reduce_weight,
    reduce_bias,
    output_cotangent,
):
    inputs = block_input[0]
    cotangent = output_cotangent[0]
    rows, width = inputs.shape
    count = lax.axis_size("ctx")
    groups = lax.axis_size("dp")
    me = lax.axis_index("ctx")
    half = rows // 2
    own_heads = -(-HEADS // count)
    share = own_heads * HEAD_DIM
    padded = share * count
    shard_rows = input_weight.shape[0]
    shard_columns = output_weight.shape[1]
    hidden = reduce_weight.shape[0] * groups
    unit = hidden // (groups * count)
    hidden_share = hidden // count
    spans = groups // count
    chunk = min(rows * count, (1 << 18) // (rows * count))

    own_expand_bias = lax.dynamic_slice_in_dim(expand_bias, me * unit, unit)
    small = jnp.stack(
        [
            attend_gain,
            attend_shift,
            query_bias,
            value_bias,
            output_bias,
            feed_gain,
            feed_shift,
            reduce_bias,
        ]
    )
    both = jnp.concatenate([small.reshape(-1), own_expand_bias])
    send_table, put_table, most = head_tables(count, width, own_heads)
    send_at = lax.dynamic_index_in_dim(jnp.asarray(send_table), me, keepdims=False)
    put_at = lax.dynamic_index_in_dim(jnp.asarray(put_table), me, keepdims=False)
    pick = (lax.broadcasted_iota(jnp.int32, (input_weight.shape[1], count * most), 0)
            == send_at[None, :]).astype(BF)
    place = (lax.broadcasted_iota(jnp.int32, (count * most, 3 * share), 1)
             == put_at[:, None]).astype(BF)
    picked = mm(input_weight, pick).astype(BF)
    arrived = exchange(
        [picked[:, step * most : (step + 1) * most] for step in range(count)], "ctx"
    )
    own_input = mm(jnp.concatenate(arrived, axis=1), place).astype(BF)
    first_part = jnp.concatenate([own_input, output_weight], axis=1)
    first_part, both = lax.optimization_barrier((first_part, both))
    first_full = lax.all_gather(first_part, "dp", axis=0, tiled=True)
    full_input = first_full[:, : 3 * share]
    output_pieces = gather_rel(first_full[:, 3 * share :], "ctx")

    expand_view = expand_weight.reshape(shard_rows, spans, count, unit)
    expand_parts = [
        expand_view[:, :, at].reshape(shard_rows, spans * unit) for at in range(count)
    ]
    reduce_view = reduce_weight.reshape(count, unit, shard_columns)
    reduce_parts = [reduce_view[at] for at in range(count)]
    paired = unit == shard_rows and spans * unit == shard_columns
    if paired:
        packs = [jnp.stack(parts) for parts in zip(expand_parts, reduce_parts)]
        packs = shuffle(exchange(shuffle(packs, me), "ctx"), me)
        full_pair = lax.all_gather(jnp.concatenate(packs, axis=2), "dp", axis=0)
        full_expand = full_pair[:, 0].reshape(width, hidden_share)
        full_reduce = full_pair[:, 1].reshape(hidden_share, width)
    else:
        expand_parts = shuffle(exchange(shuffle(expand_parts, me), "ctx"), me)
        full_expand = lax.all_gather(
            jnp.concatenate(expand_parts, axis=1), "dp", axis=0, tiled=True
        )
        reduce_parts = shuffle(exchange(shuffle(reduce_parts, me), "ctx"), me)
        full_reduce = lax.all_gather(
            jnp.concatenate(reduce_parts, axis=1), "dp", axis=0, tiled=True
        )

    gathered = gather_dp(both)
    cut = 8 * shard_rows
    vectors = gathered[:, :cut].reshape(groups, 8, shard_rows).transpose(1, 0, 2)
    vectors = vectors.reshape(8, width).astype(F32)
    own_expand = gathered[:, cut:].reshape(hidden_share).astype(F32)
    pad = padded - width
    own_query_bias = lax.dynamic_slice_in_dim(jnp.pad(vectors[2], (0, pad)), me * share, share)
    own_value_bias = lax.dynamic_slice_in_dim(jnp.pad(vectors[3], (0, pad)), me * share, share)
    proj_bias = jnp.concatenate([own_query_bias, jnp.zeros((share,), F32), own_value_bias])

    pair_list = shuffle([block_pairs[at] for at in range(count)], me)
    inner = jnp.arange(half, dtype=jnp.int32)
    positions = jnp.concatenate(
        [
            piece
            for pair in pair_list
            for piece in (pair * half + inner, (2 * count - 1 - pair) * half + inner)
        ]
    )
    row_pos = positions[:, None]
    col_pos = positions[None, :]

    normed_in, first_normed, first_inverse = layer_norm(inputs, vectors[0], vectors[1])
    attend_in = normed_in.astype(BF)
    attend_all = jnp.concatenate(gather_rel(attend_in, "ctx"))
    qkv = (mm(attend_all, full_input) + proj_bias).astype(BF)
    own_mixed, log = attend_forward(qkv, row_pos, col_pos, own_heads, chunk)
    own_mixed, output_pieces = lax.optimization_barrier((own_mixed, output_pieces))
    full_output = jnp.concatenate(shuffle(output_pieces, me), axis=1)
    mixed_parts = shuffle(
        exchange([own_mixed[at * rows : (at + 1) * rows] for at in range(count)], "ctx"), me
    )
    mixed = jnp.concatenate(mixed_parts, axis=1)[:, :width]
    mixed, cot_low = lax.optimization_barrier((mixed, cotangent.astype(BF)))
    cot_all = jnp.concatenate(gather_rel(cot_low, "ctx"))
    resid = inputs + mm(mixed, full_output) + vectors[4]
    normed_mid, second_normed, second_inverse = layer_norm(resid, vectors[5], vectors[6])
    feed_in = normed_mid.astype(BF)
    feed_all = jnp.concatenate(gather_rel(feed_in, "ctx"))
    before = mm(feed_all, full_expand) + own_expand
    activated, slope = gelu_pair(before)
    activ_low = activated.astype(BF)

    grad_before = mm_nt(cot_all, full_reduce) * slope
    before_low = grad_before.astype(BF)
    grad_expand_bias = jnp.sum(grad_before, axis=0)
    grad_feed_in = reduce_rows(mm_nt(before_low, full_expand), "ctx")
    grad_reduce = mm_tn(activ_low, cot_all).astype(BF)
    grad_expand = mm_tn(feed_all, before_low).astype(BF)
    if paired:
        pair = jnp.concatenate(
            [part.reshape(groups, unit, width) for part in (grad_reduce, grad_expand)], axis=1
        ).reshape(groups * 2 * unit, width)
        pair, grad_feed_in = lax.optimization_barrier((pair, grad_feed_in))
        pair = lax.psum_scatter(pair, "dp", scatter_dimension=0, tiled=True)
        back_reduce, back_expand = pair[:unit], pair[unit:]
    else:
        back_reduce = lax.psum_scatter(grad_reduce, "dp", scatter_dimension=0, tiled=True)
        back_expand = lax.psum_scatter(grad_expand, "dp", scatter_dimension=0, tiled=True)
    grad_mid, grad_feed_gain, grad_feed_shift = norm_backward(
        grad_feed_in, second_normed, second_inverse, vectors[5]
    )
    grad_resid = cotangent + grad_mid
    resid_low = grad_resid.astype(BF)
    grad_mixed = jnp.pad(mm_nt(resid_low, full_output).astype(BF), ((0, 0), (0, pad)))
    own_grad_mixed = jnp.concatenate(
        exchange(
            shuffle([grad_mixed[:, at * share : (at + 1) * share] for at in range(count)], me),
            "ctx",
        )
    )
    mixed_all = jnp.concatenate(gather_rel(mixed, "ctx"))
    resid_cols = jnp.concatenate(
        exchange(
            shuffle(
                [
                    resid_low[:, at * shard_columns : (at + 1) * shard_columns]
                    for at in range(count)
                ],
                me,
            ),
            "ctx",
        )
    )
    own_grad_mixed, late_activ = lax.optimization_barrier((own_grad_mixed, activ_low))
    output = resid + reduce_rows(mm(late_activ, full_reduce), "ctx") + vectors[7]

    grad_proj, proj_sums = attend_backward(
        qkv, row_pos, col_pos, log, own_mixed, own_grad_mixed, own_heads, chunk
    )
    last_grads = [mm_tn(attend_all, grad_proj), mm_tn(mixed_all, resid_cols)]
    keep, away = split_cores(jnp.concatenate(last_grads, axis=1))
    blocks = sum_cores(keep, away)
    blocks, late_proj = lax.optimization_barrier((blocks, grad_proj))
    last_total = sum_levels(blocks)
    grad_input = last_total[:, : 3 * share].astype(BF)
    grad_output_weight = last_total[:, 3 * share :]
    grad_attend_in = reduce_rows(mm_nt(late_proj, full_input), "ctx")
    grad_first, grad_attend_gain, grad_attend_shift = norm_backward(
        grad_attend_in, first_normed, first_inverse, vectors[0]
    )
    input_grad = grad_resid + grad_first

    back_input = mm_nt(grad_input, place).astype(BF)
    back_input = exchange(
        [back_input[:, step * most : (step + 1) * most] for step in range(count)], "ctx"
    )
    grad_input_weight = mm_nt(jnp.concatenate(back_input, axis=1), pick)
    back_reduce = [
        back_reduce[:, at * shard_columns : (at + 1) * shard_columns] for at in range(count)
    ]
    back_expand = [
        back_expand[:, at * spans * unit : (at + 1) * spans * unit] for at in range(count)
    ]
    if paired and spans * unit == shard_columns:
        backs = [jnp.stack(pair) for pair in zip(back_reduce, back_expand)]
        backs = shuffle(exchange(shuffle(backs, me), "ctx"), me)
        back_reduce = [piece[0] for piece in backs]
        back_expand = [piece[1] for piece in backs]
    else:
        back_reduce = shuffle(exchange(shuffle(back_reduce, me), "ctx"), me)
        back_expand = shuffle(exchange(shuffle(back_expand, me), "ctx"), me)
    grad_reduce_weight = jnp.concatenate(back_reduce, axis=0).astype(F32)
    grad_expand_weight = (
        jnp.stack([piece.reshape(shard_rows, spans, unit) for piece in back_expand], axis=2)
        .reshape(shard_rows, spans * count * unit)
        .astype(F32)
    )

    def widen(piece):
        whole = lax.dynamic_update_slice(jnp.zeros((padded,), F32), piece, (me * share,))
        return whole[:width]

    stacked = jnp.stack(
        [
            grad_attend_gain,
            grad_attend_shift,
            widen(proj_sums[0]),
            widen(proj_sums[1]),
            jnp.sum(grad_resid, axis=0),
            grad_feed_gain,
            grad_feed_shift,
            jnp.sum(cotangent, axis=0),
        ]
    )
    slots = (jnp.arange(count) == me).astype(F32)
    hidden_sums = grad_expand_bias.reshape(groups, 1, unit) * slots[None, :, None]
    vector_rows = stacked.reshape(8, groups, shard_rows).transpose(1, 0, 2).reshape(groups, -1)
    all_rows = jnp.concatenate([vector_rows, hidden_sums.reshape(groups, -1)], axis=1)
    level, core, levels = place_of_dp()
    by_core = all_rows.reshape(levels, CORES, -1)
    dp_sum = jnp.where(core == 0, by_core[:, 0], by_core[:, 1]) + swap_with(
        jnp.where(core == 0, by_core[:, 1], by_core[:, 0]), "dp", 1
    )
    dp_blocks = shuffle([dp_sum[at] for at in range(levels)], level)
    dp_total = dp_blocks[0]
    for step in range(1, levels):
        dp_total = dp_total + swap_with(dp_blocks[step], "dp", step * CORES)
    ctx_blocks = gather_rel(dp_total, "ctx")
    total = sum(ctx_blocks[1:], ctx_blocks[0])
    sums = total[:cut].reshape(8, shard_rows)
    return (
        output[None],
        input_grad[None],
        sums[0],
        sums[1],
        grad_input_weight,
        sums[2],
        sums[3],
        grad_output_weight,
        sums[4],
        sums[5],
        sums[6],
        grad_expand_weight,
        total[cut:],
        grad_reduce_weight,
        sums[7],
    )


def solution(mesh):
    matrix = P("dp", "ctx")
    vector = P("dp")
    tokens = P("dp", "ctx", None)
    return jax.shard_map(
        body,
        mesh=mesh,
        in_specs=(
            tokens,
            P(),
            vector,
            vector,
            matrix,
            vector,
            vector,
            matrix,
            vector,
            vector,
            vector,
            matrix,
            vector,
            matrix,
            vector,
            tokens,
        ),
        out_specs=(
            tokens,
            tokens,
            vector,
            vector,
            matrix,
            vector,
            vector,
            matrix,
            vector,
            vector,
            vector,
            matrix,
            vector,
            matrix,
            vector,
        ),
        check_vma=False,
    )
```

```python
import numpy as np

import jax
import jax.numpy as jnp
from jax import lax
from jax.experimental import pallas as pl
from jax.experimental.pallas import tpu as pltpu
from jax.sharding import PartitionSpec as P

HEADS = 17
HEAD_DIM = 64

EPSILON = 1e-05
GELU_ROOT = 0.7978845608028654
GELU_CUBIC = 0.044715
MASKED = -1e30
CORES = 2

BF = jnp.bfloat16
F32 = jnp.float32


def layer_norm(matrix, norm_gain, norm_shift):
    average = jnp.mean(matrix, axis=-1, keepdims=True)
    centered = matrix - average
    variance = jnp.mean(centered * centered, axis=-1, keepdims=True)
    inverse = lax.rsqrt(variance + EPSILON)
    normed = centered * inverse
    return (normed * norm_gain + norm_shift, normed, inverse)


def norm_backward(upstream, normed, inverse, norm_gain):
    grad_gain = jnp.sum(upstream * normed, axis=0)
    grad_shift = jnp.sum(upstream, axis=0)
    scaled = upstream * norm_gain
    centred_grad = (
        scaled
        - jnp.mean(scaled, axis=-1, keepdims=True)
        - normed * jnp.mean(scaled * normed, axis=-1, keepdims=True)
    )
    return (inverse * centred_grad, grad_gain, grad_shift)


def gelu_pair(before):
    cubic = GELU_ROOT * (before + GELU_CUBIC * before * before * before)
    tangent = jnp.tanh(cubic)
    result = 0.5 * before * (1.0 + tangent)
    derivative = 0.5 * (1.0 + tangent) + 0.5 * before * (1.0 - tangent * tangent) * GELU_ROOT * (
        1.0 + 3.0 * GELU_CUBIC * before * before
    )
    return (result, derivative)


def mm(left, right):
    return jnp.dot(left, right, preferred_element_type=F32)


def mm_nt(left, right):
    return lax.dot_general(left, right, (((1,), (1,)), ((), ())), preferred_element_type=F32)


def mm_tn(left, right):
    return lax.dot_general(left, right, (((0,), (0,)), ((), ())), preferred_element_type=F32)


def shuffle(blocks, me):
    blocks = list(blocks)
    step = 1
    while step < len(blocks):
        odd = (me // step) % 2 == 1
        blocks = [
            jnp.where(odd, blocks[at ^ step], blocks[at]) for at in range(len(blocks))
        ]
        step *= 2
    return blocks


def swap_with(value, axis, step):
    count = lax.axis_size(axis)
    return lax.ppermute(value, axis, [(at, at ^ step) for at in range(count)])


def exchange(blocks, axis):
    return [blocks[0]] + [
        swap_with(blocks[step], axis, step) for step in range(1, len(blocks))
    ]


def gather_rel(value, axis):
    return exchange([value] * lax.axis_size(axis), axis)


def reduce_rows(partial, axis):
    count = lax.axis_size(axis)
    rows = partial.shape[0] // count
    total = partial[:rows]
    for step in range(1, count):
        piece = partial[step * rows : (step + 1) * rows].astype(BF)
        total = total + swap_with(piece, axis, step).astype(F32)
    return total


def place_of_dp():
    index = lax.axis_index("dp")
    return index // CORES, index % CORES, lax.axis_size("dp") // CORES


def gather_levels(value):
    level, _, levels = place_of_dp()
    blocks = [value] + [swap_with(value, "dp", CORES * step) for step in range(1, levels)]
    return jnp.stack(shuffle(blocks, level))


def gather_dp(value):
    _, core, levels = place_of_dp()
    mine = gather_levels(value)
    other = swap_with(mine, "dp", 1)
    first = jnp.where(core == 0, mine, other)
    second = jnp.where(core == 0, other, mine)
    return jnp.stack([first, second], axis=1).reshape((CORES * levels,) + value.shape)


def split_cores(grad):
    _, core, levels = place_of_dp()
    view = grad.reshape(levels, CORES, -1, grad.shape[1])
    keep = jnp.where(core == 0, view[:, 0], view[:, 1])
    away = jnp.where(core == 0, view[:, 1], view[:, 0]).astype(BF)
    return keep, away


def sum_cores(keep, away):
    level, _, levels = place_of_dp()
    keep = keep + swap_with(away, "dp", 1).astype(F32)
    blocks = shuffle([keep[at] for at in range(levels)], level)
    return blocks[:1] + [block.astype(BF) for block in blocks[1:]]


def sum_levels(blocks):
    total = blocks[0]
    for step in range(1, len(blocks)):
        total = total + swap_with(blocks[step], "dp", step * CORES).astype(F32)
    return total


def head_tables(count, width, own_heads):
    share = own_heads * HEAD_DIM
    columns = 3 * width // count
    lists = {}
    most = 1
    for target in range(count):
        for place in range(3 * share):
            part, inner = divmod(place, share)
            column = target * share + inner
            if column < width:
                source, local = divmod(part * width + column, columns)
                lists.setdefault((source, target), []).append((local, place))
    most = max(len(entries) for entries in lists.values())
    send = np.full((count, count, most), -1, np.int32)
    put = np.full((count, count, most), -1, np.int32)
    for (source, target), entries in lists.items():
        for at, (local, place) in enumerate(entries):
            send[source, source ^ target, at] = local
            put[target, source ^ target, at] = place
    return send.reshape(count, -1), put.reshape(count, -1), most


def scores_of(query, key, row_pos, col_pos):
    score = mm_nt(query, key) * (HEAD_DIM ** (-0.5))
    return jnp.where(col_pos <= row_pos, score, MASKED)


def attend_kernel(own_heads, chunk, qkv_ref, row_ref, col_ref, mixed_ref, log_ref):
    rows = qkv_ref.shape[0]
    share = own_heads * HEAD_DIM
    col_pos = col_ref[...]
    for head in range(own_heads):
        span = slice(head * HEAD_DIM, (head + 1) * HEAD_DIM)
        key = qkv_ref[:, share + head * HEAD_DIM : share + (head + 1) * HEAD_DIM]
        value = qkv_ref[:, 2 * share + head * HEAD_DIM : 2 * share + (head + 1) * HEAD_DIM]
        for first in range(0, rows, chunk):
            part = slice(first, first + chunk)
            score = scores_of(qkv_ref[part, span], key, row_ref[part, :], col_pos)
            top = jnp.max(score, axis=-1, keepdims=True)
            log = top + jnp.log(jnp.sum(jnp.exp(score - top), axis=-1, keepdims=True))
            probs = jnp.exp(score - log).astype(BF)
            mixed_ref[part, span] = mm(probs, value).astype(BF)
            log_ref[part, head : head + 1] = log


def attend_back_kernel(
    own_heads, chunk, qkv_ref, row_ref, col_ref, log_ref, mixed_ref, grad_ref, out_ref, bias_ref
):
    rows = qkv_ref.shape[0]
    share = own_heads * HEAD_DIM
    scale = HEAD_DIM ** (-0.5)
    col_pos = col_ref[...]
    for head in range(own_heads):
        span = slice(head * HEAD_DIM, (head + 1) * HEAD_DIM)
        key_span = slice(share + head * HEAD_DIM, share + (head + 1) * HEAD_DIM)
        value_span = slice(2 * share + head * HEAD_DIM, 2 * share + (head + 1) * HEAD_DIM)
        key = qkv_ref[:, key_span]
        value = qkv_ref[:, value_span]
        grad_key = grad_value = grad_query_sum = None
        for first in range(0, rows, chunk):
            part = slice(first, first + chunk)
            query = qkv_ref[part, span]
            score = scores_of(query, key, row_ref[part, :], col_pos)
            exact = jnp.exp(score - log_ref[part, head : head + 1])
            grad = grad_ref[part, span]
            delta = jnp.sum(
                grad.astype(F32) * mixed_ref[part, span].astype(F32), axis=-1, keepdims=True
            )
            new_value = mm_tn(exact.astype(BF), grad)
            grad_score = (exact * (mm_nt(grad, value) - delta) * scale).astype(BF)
            grad_query = mm(grad_score, key)
            new_key = mm_tn(grad_score, query)
            new_sum = jnp.sum(grad_query, axis=0, keepdims=True)
            out_ref[part, span] = grad_query.astype(BF)
            if first == 0:
                grad_key, grad_value, grad_query_sum = new_key, new_value, new_sum
            else:
                grad_key = grad_key + new_key
                grad_value = grad_value + new_value
                grad_query_sum = grad_query_sum + new_sum
        out_ref[:, key_span] = grad_key.astype(BF)
        out_ref[:, value_span] = grad_value.astype(BF)
        bias_ref[0:1, span] = grad_query_sum
        bias_ref[1:2, span] = jnp.sum(grad_value, axis=0, keepdims=True)


def attend_forward(qkv, row_pos, col_pos, own_heads, chunk):
    rows = qkv.shape[0]
    return pl.pallas_call(
        lambda *refs: attend_kernel(own_heads, chunk, *refs),
        out_shape=(
            jax.ShapeDtypeStruct((rows, own_heads * HEAD_DIM), BF),
            jax.ShapeDtypeStruct((rows, own_heads), F32),
        ),
        name="attend",
    )(qkv, row_pos, col_pos)


def attend_backward(qkv, row_pos, col_pos, log, mixed, grad, own_heads, chunk):
    rows = qkv.shape[0]
    return pl.pallas_call(
        lambda *refs: attend_back_kernel(own_heads, chunk, *refs),
        out_shape=(
            jax.ShapeDtypeStruct((rows, 3 * own_heads * HEAD_DIM), BF),
            jax.ShapeDtypeStruct((2, own_heads * HEAD_DIM), F32),
        ),
        name="attend_back",
    )(qkv, row_pos, col_pos, log, mixed, grad)


def body(
    block_input,
    block_pairs,
    attend_gain,
    attend_shift,
    input_weight,
    query_bias,
    value_bias,
    output_weight,
    output_bias,
    feed_gain,
    feed_shift,
    expand_weight,
    expand_bias,
    reduce_weight,
    reduce_bias,
    output_cotangent,
):
    inputs = block_input[0]
    cotangent = output_cotangent[0]
    rows, width = inputs.shape
    count = lax.axis_size("ctx")
    groups = lax.axis_size("dp")
    me = lax.axis_index("ctx")
    half = rows // 2
    own_heads = -(-HEADS // count)
    share = own_heads * HEAD_DIM
    padded = share * count
    shard_rows = input_weight.shape[0]
    shard_columns = output_weight.shape[1]
    hidden = reduce_weight.shape[0] * groups
    unit = hidden // (groups * count)
    hidden_share = hidden // count
    spans = groups // count
    chunk = min(rows * count, (1 << 18) // (rows * count))

    own_expand_bias = lax.dynamic_slice_in_dim(expand_bias, me * unit, unit)
    small = jnp.stack(
        [
            attend_gain,
            attend_shift,
            query_bias,
            value_bias,
            output_bias,
            feed_gain,
            feed_shift,
            reduce_bias,
        ]
    )
    both = jnp.concatenate([small.reshape(-1), own_expand_bias])
    send_table, put_table, most = head_tables(count, width, own_heads)
    send_at = lax.dynamic_index_in_dim(jnp.asarray(send_table), me, keepdims=False)
    put_at = lax.dynamic_index_in_dim(jnp.asarray(put_table), me, keepdims=False)
    pick = (lax.broadcasted_iota(jnp.int32, (input_weight.shape[1], count * most), 0)
            == send_at[None, :]).astype(BF)
    place = (lax.broadcasted_iota(jnp.int32, (count * most, 3 * share), 1)
             == put_at[:, None]).astype(BF)
    picked = mm(input_weight, pick).astype(BF)
    arrived = exchange(
        [picked[:, step * most : (step + 1) * most] for step in range(count)], "ctx"
    )
    output_parts = shuffle(gather_rel(output_weight, "ctx"), me)
    own_input = mm(jnp.concatenate(arrived, axis=1), place).astype(BF)
    gap = -3 * share % 128
    first_part = jnp.concatenate(
        [jnp.pad(own_input, ((0, 0), (0, gap)))] + output_parts, axis=1
    )
    first_part, both = lax.optimization_barrier((first_part, both))
    first_full = lax.all_gather(first_part, "dp", axis=0, tiled=True)
    full_input = first_full[:, : 3 * share]
    full_output = first_full[:, 3 * share + gap :]

    expand_view = expand_weight.reshape(shard_rows, spans, count, unit)
    expand_parts = [
        expand_view[:, :, at].reshape(shard_rows, spans * unit) for at in range(count)
    ]
    reduce_view = reduce_weight.reshape(count, unit, shard_columns)
    reduce_parts = [reduce_view[at] for at in range(count)]
    paired = unit == shard_rows and spans * unit == shard_columns
    if paired:
        packs = [jnp.stack(parts) for parts in zip(expand_parts, reduce_parts)]
        packs = shuffle(exchange(shuffle(packs, me), "ctx"), me)
        full_pair = lax.all_gather(jnp.concatenate(packs, axis=2), "dp", axis=0)
        full_expand = full_pair[:, 0].reshape(width, hidden_share)
        full_reduce = full_pair[:, 1].reshape(hidden_share, width)
    else:
        expand_parts = shuffle(exchange(shuffle(expand_parts, me), "ctx"), me)
        full_expand = lax.all_gather(
            jnp.concatenate(expand_parts, axis=1), "dp", axis=0, tiled=True
        )
        reduce_parts = shuffle(exchange(shuffle(reduce_parts, me), "ctx"), me)
        full_reduce = lax.all_gather(
            jnp.concatenate(reduce_parts, axis=1), "dp", axis=0, tiled=True
        )

    gathered = gather_dp(both)
    cut = 8 * shard_rows
    vectors = gathered[:, :cut].reshape(groups, 8, shard_rows).transpose(1, 0, 2)
    vectors = vectors.reshape(8, width).astype(F32)
    own_expand = gathered[:, cut:].reshape(hidden_share).astype(F32)
    pad = padded - width
    own_query_bias = lax.dynamic_slice_in_dim(jnp.pad(vectors[2], (0, pad)), me * share, share)
    own_value_bias = lax.dynamic_slice_in_dim(jnp.pad(vectors[3], (0, pad)), me * share, share)
    proj_bias = jnp.concatenate([own_query_bias, jnp.zeros((share,), F32), own_value_bias])

    pair_list = shuffle([block_pairs[at] for at in range(count)], me)
    inner = jnp.arange(half, dtype=jnp.int32)
    positions = jnp.concatenate(
        [
            piece
            for pair in pair_list
            for piece in (pair * half + inner, (2 * count - 1 - pair) * half + inner)
        ]
    )
    row_pos = positions[:, None]
    col_pos = positions[None, :]

    normed_in, first_normed, first_inverse = layer_norm(inputs, vectors[0], vectors[1])
    attend_in = normed_in.astype(BF)
    attend_all = jnp.concatenate(gather_rel(attend_in, "ctx"))
    qkv = (mm(attend_all, full_input) + proj_bias).astype(BF)
    own_mixed, log = attend_forward(qkv, row_pos, col_pos, own_heads, chunk)
    mixed_parts = shuffle(
        exchange([own_mixed[at * rows : (at + 1) * rows] for at in range(count)], "ctx"), me
    )
    mixed = jnp.concatenate(mixed_parts, axis=1)[:, :width]
    mixed, cot_low = lax.optimization_barrier((mixed, cotangent.astype(BF)))
    cot_all = jnp.concatenate(gather_rel(cot_low, "ctx"))
    resid = inputs + mm(mixed, full_output) + vectors[4]
    normed_mid, second_normed, second_inverse = layer_norm(resid, vectors[5], vectors[6])
    feed_in = normed_mid.astype(BF)
    feed_all = jnp.concatenate(gather_rel(feed_in, "ctx"))
    before = mm(feed_all, full_expand) + own_expand
    activated, slope = gelu_pair(before)
    activ_low, mixed_all = lax.optimization_barrier(
        (activated.astype(BF), jnp.concatenate(gather_rel(mixed, "ctx")))
    )

    grad_before = mm_nt(cot_all, full_reduce) * slope
    before_low = grad_before.astype(BF)
    grad_expand_bias = jnp.sum(grad_before, axis=0)
    grad_feed_in = reduce_rows(mm_nt(before_low, full_expand), "ctx")
    grad_reduce = mm_tn(activ_low, cot_all).astype(BF)
    grad_expand = mm_tn(feed_all, before_low).astype(BF)
    if paired:
        pair = jnp.concatenate(
            [part.reshape(groups, unit, width) for part in (grad_reduce, grad_expand)], axis=1
        ).reshape(groups * 2 * unit, width)
        pair, grad_feed_in = lax.optimization_barrier((pair, grad_feed_in))
        pair = lax.psum_scatter(pair, "dp", scatter_dimension=0, tiled=True)
        pair = (pair[:unit], pair[unit:])
    else:
        pair = (
            lax.psum_scatter(grad_reduce, "dp", scatter_dimension=0, tiled=True),
            lax.psum_scatter(grad_expand, "dp", scatter_dimension=0, tiled=True),
        )
    grad_mid, grad_feed_gain, grad_feed_shift = norm_backward(
        grad_feed_in, second_normed, second_inverse, vectors[5]
    )
    grad_resid = cotangent + grad_mid
    resid_low = grad_resid.astype(BF)
    grad_mixed = jnp.pad(mm_nt(resid_low, full_output).astype(BF), ((0, 0), (0, pad)))
    own_grad_mixed = jnp.concatenate(
        exchange(
            shuffle([grad_mixed[:, at * share : (at + 1) * share] for at in range(count)], me),
            "ctx",
        )
    )
    resid_cols = jnp.concatenate(
        exchange(
            shuffle(
                [
                    resid_low[:, at * shard_columns : (at + 1) * shard_columns]
                    for at in range(count)
                ],
                me,
            ),
            "ctx",
        )
    )
    output_blocks = sum_cores(*split_cores(mm_tn(mixed_all, resid_cols)))

    grad_proj, proj_sums = attend_backward(
        qkv, row_pos, col_pos, log, own_mixed, own_grad_mixed, own_heads, chunk
    )
    keep_input, away_input = split_cores(mm_tn(attend_all, grad_proj))
    away_input, late_activ = lax.optimization_barrier((away_input, activ_low))
    input_blocks = sum_cores(keep_input, away_input)
    partial_output = mm(late_activ, full_reduce)
    blocks, late_proj, partial_output = lax.optimization_barrier(
        (
            [
                jnp.concatenate(both_blocks, axis=1)
                for both_blocks in zip(input_blocks, output_blocks)
            ],
            grad_proj,
            partial_output,
        )
    )
    last_total = sum_levels(blocks)
    grad_input = last_total[:, : 3 * share].astype(BF)
    grad_output_weight = last_total[:, 3 * share :]
    grad_attend_in = reduce_rows(mm_nt(late_proj, full_input), "ctx")
    grad_attend_in, partial_output = lax.optimization_barrier((grad_attend_in, partial_output))
    output = resid + reduce_rows(partial_output, "ctx") + vectors[7]
    grad_first, grad_attend_gain, grad_attend_shift = norm_backward(
        grad_attend_in, first_normed, first_inverse, vectors[0]
    )
    input_grad = grad_resid + grad_first

    def widen(piece):
        whole = lax.dynamic_update_slice(jnp.zeros((padded,), F32), piece, (me * share,))
        return whole[:width]

    stacked = jnp.stack(
        [
            grad_attend_gain,
            grad_attend_shift,
            widen(proj_sums[0]),
            widen(proj_sums[1]),
            jnp.sum(grad_resid, axis=0),
            grad_feed_gain,
            grad_feed_shift,
            jnp.sum(cotangent, axis=0),
        ]
    )
    slots = (jnp.arange(count) == me).astype(F32)
    hidden_sums = grad_expand_bias.reshape(groups, 1, unit) * slots[None, :, None]
    vector_rows = stacked.reshape(8, groups, shard_rows).transpose(1, 0, 2).reshape(groups, -1)
    all_rows = jnp.concatenate([vector_rows, hidden_sums.reshape(groups, -1)], axis=1)
    level, core, levels = place_of_dp()
    by_core = all_rows.reshape(levels, CORES, -1)
    dp_sum = jnp.where(core == 0, by_core[:, 0], by_core[:, 1]) + swap_with(
        jnp.where(core == 0, by_core[:, 1], by_core[:, 0]), "dp", 1
    )
    dp_blocks = shuffle([dp_sum[at] for at in range(levels)], level)
    dp_total = dp_blocks[0]
    for step in range(1, levels):
        dp_total = dp_total + swap_with(dp_blocks[step], "dp", step * CORES)
    dp_total, pair = lax.optimization_barrier((dp_total, pair))
    back_reduce, back_expand = pair
    ctx_blocks = gather_rel(dp_total, "ctx")
    total = sum(ctx_blocks[1:], ctx_blocks[0])
    sums = total[:cut].reshape(8, shard_rows)
    back_input = mm_nt(grad_input, place).astype(BF)
    back_input = exchange(
        [back_input[:, step * most : (step + 1) * most] for step in range(count)], "ctx"
    )
    grad_input_weight = mm_nt(jnp.concatenate(back_input, axis=1), pick)
    back_reduce = [
        back_reduce[:, at * shard_columns : (at + 1) * shard_columns] for at in range(count)
    ]
    back_expand = [
        back_expand[:, at * spans * unit : (at + 1) * spans * unit] for at in range(count)
    ]
    if paired and spans * unit == shard_columns:
        backs = [jnp.stack(pair) for pair in zip(back_reduce, back_expand)]
        backs = shuffle(exchange(shuffle(backs, me), "ctx"), me)
        back_reduce = [piece[0] for piece in backs]
        back_expand = [piece[1] for piece in backs]
    else:
        back_reduce = shuffle(exchange(shuffle(back_reduce, me), "ctx"), me)
        back_expand = shuffle(exchange(shuffle(back_expand, me), "ctx"), me)
    grad_reduce_weight = jnp.concatenate(back_reduce, axis=0).astype(F32)
    grad_expand_weight = (
        jnp.stack([piece.reshape(shard_rows, spans, unit) for piece in back_expand], axis=2)
        .reshape(shard_rows, spans * count * unit)
        .astype(F32)
    )

    return (
        output[None],
        input_grad[None],
        sums[0],
        sums[1],
        grad_input_weight,
        sums[2],
        sums[3],
        grad_output_weight,
        sums[4],
        sums[5],
        sums[6],
        grad_expand_weight,
        total[cut:],
        grad_reduce_weight,
        sums[7],
    )


def solution(mesh):
    matrix = P("dp", "ctx")
    vector = P("dp")
    tokens = P("dp", "ctx", None)
    return jax.shard_map(
        body,
        mesh=mesh,
        in_specs=(
            tokens,
            P(),
            vector,
            vector,
            matrix,
            vector,
            vector,
            matrix,
            vector,
            vector,
            vector,
            matrix,
            vector,
            matrix,
            vector,
            tokens,
        ),
        out_specs=(
            tokens,
            tokens,
            vector,
            vector,
            matrix,
            vector,
            vector,
            matrix,
            vector,
            vector,
            vector,
            matrix,
            vector,
            matrix,
            vector,
        ),
        check_vma=False,
    )
```
